512 devices in a mesh: seq: 64 (over x, z), head: 8 (over y, core).
Axes of the slice: x: 4, y: 4, z: 16, core: 2. Of those that a mesh axis runs over, the one named last changes fastest.
Arguments:
- queries: bfloat16 [45056, 4096], P(('seq', 'head')), may hold values from -64 to 64
- database_rows: bfloat16 [512, 64, 896], P('seq', 'head'), may hold values from -6 to 6
- w_encoder: bfloat16 [896, 896], P('seq'), may hold values from -0.1875 to 0.1875
- w_key: bfloat16 [896, 4096], P(None, 'head'), may hold values from -0.1875 to 0.1875
- w_value: bfloat16 [896, 4096], P(None, 'head'), may hold values from -0.1875 to 0.1875
- neighbour_ids: int32 [704, 2], replicated, may hold values from 0 to 511, as said below
Outputs:
- attended: bfloat16 [45056, 4096], P(('seq', 'head'))
The draws below stay inside these ranges and needn't reach their ends.
Inputs may be any that keep to these rules, and one draw needn't show every extreme that they name: `neighbour_ids`: among the 22 neighbours of the spans of one sequence shard (rows s * 11 onward), at most 2 are entries of any one database shard, and in every shard some database shard holds exactly 2 of them. The same entry may appear more than once.
All inputs are finite; a program needn't handle non-finite values.
Results may differ from the reference program's by a relative error of at most 0.012.
The reference program's roundings to bfloat16 on the way (of `normed`, `encoded` and `probs`) count: a program that leaves them out, or rounds other values in their place, can miss the bound.
Values may be sent and summed in bfloat16 or wider, within the bound.
A program may use at most 64 MiB of HBM per device.

```python
import jax
import jax.numpy as jnp
from jax import lax

D = 4096
HEADS = 32
HEAD_DIM = 128
ENC = 896
SPAN = 64
NBR_LEN = 64
K_NBR = 2
DB_DEV = 8
TOKENS = 45056
SPANS = 704
DB = 512
NBR_DEV = 22
CAP = 2


def draw_queries(key, part):
    first = jax.random.fold_in(jax.random.fold_in(key, 11), 0)
    drawn = jax.random.normal(first, (TOKENS, D), jnp.float32)
    return jnp.clip(drawn, -64.0, 64.0).astype(jnp.bfloat16)


def draw_neighbour_ids(key, part):
    shard_owner_count = DB // DB_DEV
    block_count = SPANS * K_NBR // NBR_DEV
    slot_grand_total = shard_owner_count * CAP
    first, second, third, fourth = jax.random.split(jax.random.fold_in(key, 23), 4)
    popular_position = jax.random.permutation(first, shard_owner_count).astype(jnp.int32)
    slot_shard_owner = jnp.repeat(jnp.arange(shard_owner_count, dtype=jnp.int32), CAP)
    extra_reward = (shard_owner_count - popular_position[slot_shard_owner]) * (2 * (2 ** 20 // shard_owner_count))
    extra_reward = extra_reward + jnp.where(popular_position[slot_shard_owner] == 0, 2 ** 23, 0)
    random_jitter = jax.random.randint(second, (block_count, slot_grand_total), 0, 2 ** 20)
    ranking_score = (random_jitter + extra_reward[None, :]) * slot_grand_total + jnp.arange(slot_grand_total, dtype=jnp.int32)[None, :]
    picked_score, picked = lax.top_k(ranking_score, NBR_DEV)
    owners = slot_shard_owner[picked]
    shuffle_score = jax.random.randint(third, (block_count, NBR_DEV), 0, 2 ** 20) * NBR_DEV + jnp.arange(NBR_DEV, dtype=jnp.int32)[None, :]
    order = jnp.argsort(shuffle_score, axis=1)
    owners = jnp.take_along_axis(owners, order, axis=1)
    local_entry = jax.random.randint(fourth, (block_count, NBR_DEV), 0, DB_DEV)
    return (owners * DB_DEV + local_entry).reshape(SPANS, K_NBR).astype(jnp.int32)


def shard_levels(own_key, dims, shards, least, high):
    loudness, own = 1.0, jax.random.fold_in(own_key, 6)
    for position, shards_of in shards:
        heights = jnp.exp(jax.random.uniform(jax.random.fold_in(own, position), (shards_of,), jnp.float32, least / len(shards), high / len(shards)))
        loudness = loudness * jnp.repeat(heights, dims[position] // shards_of).reshape([-1 if axis == position else 1 for axis in range(len(dims))])
    return loudness


def gaussian(key, extent, deviation, most, pieces=(), kind=jnp.bfloat16):
    entries = deviation * jax.random.normal(key, extent, jnp.float32)
    if pieces:
        entries = entries * shard_levels(key, extent, pieces, -0.22, 0.18)
    return jnp.clip(entries, -most, most).astype(kind)


def setup_inputs(seed: int = 0) -> dict:
    arg_keys = jax.random.split(jax.random.key(seed), 7)
    return {
        "queries": draw_queries(jax.random.fold_in(arg_keys[6], 71), 0),
        "database_rows": gaussian(arg_keys[1], (DB, NBR_LEN, ENC), 1.0, 6.0, ((0, 64), (1, 8))),
        "w_encoder": gaussian(arg_keys[2], (ENC, ENC), ENC ** -0.5, 0.1875, ((0, 64),)),
        "w_key": gaussian(arg_keys[3], (ENC, D), ENC ** -0.5, 0.1875, ((1, 8),)),
        "w_value": gaussian(arg_keys[4], (ENC, D), ENC ** -0.5, 0.1875, ((1, 8),)),
        "neighbour_ids": draw_neighbour_ids(jax.random.fold_in(arg_keys[6], 71), 0),
    }


def encode(raw_rows, w_encoder):
    values_in = raw_rows.astype(jnp.float32)
    mean_square = lax.optimization_barrier(jnp.mean(values_in * values_in, axis=-1, keepdims=True))
    normed = (values_in * lax.rsqrt(mean_square + 1e-06)).astype(jnp.bfloat16)
    summed = jnp.dot(normed.reshape(-1, values_in.shape[-1]), w_encoder, preferred_element_type=jnp.float32)
    return (values_in + jax.nn.silu(summed.reshape(values_in.shape))).astype(jnp.bfloat16)

def attend(query_block, key_block, value_block):
    scores = jnp.einsum('cqhd,ckhd->chqk', query_block.astype(jnp.float32), key_block.astype(jnp.float32)) * HEAD_DIM ** (-0.5)
    highest = lax.optimization_barrier(jnp.max(scores, axis=-1, keepdims=True))
    weights = jnp.exp(scores - highest)
    probs = (weights / lax.optimization_barrier(jnp.sum(weights, axis=-1, keepdims=True))).astype(jnp.bfloat16)
    mixed = jnp.einsum('chqk,ckhd->cqhd', probs.astype(jnp.float32), value_block.astype(jnp.float32))
    return mixed.astype(jnp.bfloat16)

def reference(queries, database_rows, w_encoder, w_key, w_value, neighbour_ids):
    encoded = encode(database_rows, w_encoder)
    flat_rows = encoded.reshape(-1, ENC)
    all_keys = jnp.dot(flat_rows, w_key, preferred_element_type=jnp.float32).astype(jnp.bfloat16).reshape(DB, NBR_LEN, D)
    all_values = jnp.dot(flat_rows, w_value, preferred_element_type=jnp.float32).astype(jnp.bfloat16).reshape(DB, NBR_LEN, D)
    query_spans = queries.reshape(SPANS, 1, SPAN, HEADS, HEAD_DIM)

    def one_span(inputs):
        query_block, entry_ids = inputs
        key_block = all_keys[entry_ids].reshape(1, K_NBR * NBR_LEN, HEADS, HEAD_DIM)
        value_block = all_values[entry_ids].reshape(1, K_NBR * NBR_LEN, HEADS, HEAD_DIM)
        return attend(query_block, key_block, value_block)
    attended = lax.map(one_span, (query_spans, neighbour_ids))
    return attended.reshape(TOKENS, D)
```

```python
import functools

import jax
import jax.numpy as jnp
from jax import lax
from jax.experimental import pallas as pl
from jax.experimental.pallas import tpu as pltpu
from jax.sharding import Mesh
from jax.sharding import PartitionSpec as P

HEAD_DIM = 128
SPAN = 64
NX, NZ, NY, NC = 4, 16, 4, 2
SEQ = ("x", "z")
HEAD = ("y", "c")
SEQ_HEAD = ("x", "z", "y", "c")
MESH = pl.DeviceIdType.MESH
BF16 = jnp.bfloat16
F32 = jnp.float32

ENC = 896
ENTRIES = 8
TOK = 8
SLOTS = 22
SUB = 4
WROWS = 14
COLS = 512
ROWS = 88
CHUNKS = 8
TILES = 8
GROUPS = ((0, 11),)


def kernel(
    tab_ref, db_ref, wsh_ref, q_ref, wk_ref, wv_ref, out_ref,
    zbuf, wz, wenc, wk, wv, qbuf, s_a, s_b, s_c, r_a, r_b, r_c, nb, enc, kbuf, vbuf, obuf,
    z_send, z_recv, wz_send, wz_recv, local, q_send, q_recv,
    wx_send, wx_recv, wy_send, wy_recv, wy_sib, x_send, x_recv,
    y_send, y_recv, y_sib, o_send, o_recv,
):
    x, z, y, c = (lax.axis_index(a) for a in ("x", "z", "y", "c"))
    r = 1 - 2 * c
    h = 2 * y + c

    def wrap(v, n):
        return lax.rem(v + 2 * n, n)

    def copy(src, dst, ssem, rsem, dev):
        return pltpu.make_async_remote_copy(
            src_ref=src, dst_ref=dst, send_sem=ssem, recv_sem=rsem,
            device_id=dev, device_id_type=MESH,
        )

    here = (x, z, y, c)
    sibling = (x, z, y, 1 - c)

    def at_x(dx):
        return (wrap(x + dx, NX), z, y, c)

    def at_z(dz):
        return (x, wrap(z + dz, NZ), y, c)

    def at_y(dy):
        return (x, z, wrap(y + dy, NY), c)

    others = [(0, 1)] + [(dy, e) for dy in (2, 1, 3) for e in (0, 1)]

    def at_head(dy, e):
        return (x, z, wrap(y + dy, NY), wrap(c + e, NC))

    barrier = pltpu.get_barrier_semaphore()
    partners = [at_z(1), at_z(-1), at_x(1), at_x(2), at_x(3)] + [at_head(*o) for o in others]
    for dev in partners:
        pl.semaphore_signal(barrier, inc=1, device_id=dev, device_id_type=MESH)
    pl.semaphore_wait(barrier, len(partners))

    def zpiece(owner, i):
        return zbuf.at[pl.ds(owner * ENTRIES + i * (ENTRIES // SUB), ENTRIES // SUB)]

    sends = []

    def go(cp):
        cp.start()
        sends.append(cp)

    for d in range(2):
        dev = at_z(r if d == 0 else -r)
        go(copy(wsh_ref.at[h], wz.at[x, z], wz_send.at[d, 0], wz_recv.at[d, 0], dev))
    for i in range(SUB):
        for d in range(2):
            dev = at_z(r if d == 0 else -r)
            go(copy(
                db_ref.at[pl.ds(i * (ENTRIES // SUB), ENTRIES // SUB)], zpiece(z, i),
                z_send.at[d, 0, i], z_recv.at[d, 0, i], dev,
            ))

    for n, (dy, e) in enumerate(others):
        dev = at_head(dy, e)
        to = 2 * dev[2] + dev[3]
        cols = pl.ds(pl.multiple_of(to * COLS, COLS), COLS)
        go(copy(q_ref.at[:, cols], qbuf.at[h], q_send.at[n], q_recv.at[h], dev))

    own_cols = pl.ds(pl.multiple_of(h * COLS, COLS), COLS)
    locals_ = [
        pltpu.make_async_copy(db_ref, zbuf.at[pl.ds(z * ENTRIES, ENTRIES)], local.at[0]),
        pltpu.make_async_copy(wsh_ref.at[h], wz.at[x, z], local.at[1]),
        pltpu.make_async_copy(wk_ref, wk, local.at[2]),
        pltpu.make_async_copy(wv_ref, wv, local.at[3]),
        pltpu.make_async_copy(q_ref.at[:, own_cols], qbuf.at[h], local.at[4]),
    ]
    for cp in locals_:
        cp.start()

    def z_arrive(d, k, forward):
        way = r if d == 0 else -r
        owner = wrap(z - way * (1 + k), NZ)
        dev = at_z(way)
        piece = wz.at[x, owner]
        copy(piece, piece, wz_send.at[d, k], wz_recv.at[d, k], dev).wait_recv()
        if forward:
            copy(piece, piece, wz_send.at[d, k + 1], wz_recv.at[d, k + 1], dev).start()

        def part(i):
            piece = zpiece(owner, i)
            copy(piece, piece, z_send.at[d, k, i], z_recv.at[d, k, i], dev).wait_recv()
            if forward:
                copy(piece, piece, z_send.at[d, k + 1, i], z_recv.at[d, k + 1, i], dev).start()

        return part

    def z_step(k, forwards):
        parts = [z_arrive(d, k, f) for d, f in forwards]
        for i in range(SUB):
            for part in parts:
                part(i)

    hops = (NZ // 2, NZ // 2 - 1)

    @pl.loop(0, hops[1] - 1)
    def _(k):
        z_step(k, ((0, True), (1, True)))

    z_step(hops[1] - 1, ((0, True), (1, False)))
    z_step(hops[0] - 1, ((0, False),))

    locals_[0].wait()
    locals_[1].wait()

    for n in range(1, NX):
        go(copy(wz.at[x], wz.at[x], wx_send.at[n], wx_recv.at[x], at_x(n)))

    def entry(dest, j):
        n = tab_ref[dest, j]
        return zbuf[n & (NZ * ENTRIES - 1)], n >> 7

    def slots(g):
        return range(2 * GROUPS[g][0], 2 * GROUPS[g][1])

    def slot_ds(g):
        a, b = GROUPS[g]
        return pl.ds(2 * a, 2 * (b - a))

    n_groups = len(GROUPS)
    far, near = wrap(x + 2 * r, NX), wrap(x - r, NX)
    ahead = wrap(x + r, NX)
    for g in range(n_groups):
        for j in slots(g):
            s_a[j] = entry(far, j)[0]
        go(copy(s_a.at[slot_ds(g)], r_a.at[slot_ds(g)], x_send.at[0, g], x_recv.at[0, g], at_x(r)))
        for j in slots(g):
            s_b[j] = entry(near, j)[0]
        go(copy(s_b.at[slot_ds(g)], r_b.at[slot_ds(g)], x_send.at[1, g], x_recv.at[1, g], at_x(-r)))

    for n in range(1, NX):
        src = wrap(x + n, NX)
        copy(wz.at[src], wz.at[src], wx_send.at[n], wx_recv.at[src], at_x(n)).wait_recv()
    lhs_rows, rhs_rows = ENTRIES * WROWS, ENTRIES * 16
    row = lax.broadcasted_iota(jnp.int32, (lhs_rows, rhs_rows), 0)
    col = lax.broadcasted_iota(jnp.int32, (lhs_rows, rhs_rows), 1)
    inner = col & 15
    pick = jnp.where((inner < WROWS) & ((col >> 4) * WROWS + inner == row), 1.0, 0.0).astype(BF16)
    for a in range(NX):
        for b in range(2):
            block = wz[a, pl.ds(b * ENTRIES, ENTRIES)].reshape(rhs_rows, 128)
            packed = jnp.dot(pick, block, preferred_element_type=F32).astype(BF16)
            wenc[h, pl.ds((2 * a + b) * lhs_rows, lhs_rows), :] = packed

    class Gather:
        def __init__(self, region, send, recv, sib):
            self.region, self.send, self.recv, self.sib = region, send, recv, sib

        def start(self):
            own = self.region(h)
            go(copy(own, own, self.send(0), self.recv(0), at_y(r)))
            go(copy(own, own, self.send(1), self.recv(1), at_y(-r)))
            go(copy(own, own, self.send(2), self.sib(0), sibling))

        def arrive(self, n):
            step = (-1, 1, 2)[n] * r
            src = wrap(y + step, NY)
            piece = self.region(2 * src + c)
            copy(piece, piece, self.send(0), self.recv(n), at_y(r)).wait_recv()
            if n == 0:
                go(copy(piece, piece, self.send(3), self.recv(2), at_y(r)))
            go(copy(piece, piece, self.send(4 + n), self.sib(wrap(step, NY)), sibling))

        def from_sibling(self, delta):
            src = wrap(y + delta, NY)
            piece = self.region(2 * src + 1 - c)
            copy(piece, piece, self.send(0), self.sib(delta), sibling).wait_recv()

    w_gather = Gather(
        lambda t: wenc.at[t], lambda n: wy_send.at[n], lambda n: wy_recv.at[n], lambda n: wy_sib.at[n]
    )
    w_gather.start()

    for g in range(n_groups):
        copy(s_a.at[slot_ds(g)], r_a.at[slot_ds(g)], x_send.at[0, g], x_recv.at[0, g], at_x(r)).wait_recv()
        for j in slots(g):
            mine, col_of = entry(ahead, j)
            s_c[j] = jnp.where(col_of == x, mine, r_a[j])
        go(copy(s_c.at[slot_ds(g)], r_c.at[slot_ds(g)], x_send.at[2, g], x_recv.at[2, g], at_x(r)))

    for n in range(3):
        w_gather.arrive(n)
    for n in range(NY):
        w_gather.from_sibling(n)

    gathers = []
    for g in range(n_groups):
        a, b = GROUPS[g]
        count = 2 * (b - a)
        rows = pl.ds(16 * a, 16 * (b - a))
        copy(s_b.at[slot_ds(g)], r_b.at[slot_ds(g)], x_send.at[1, g], x_recv.at[1, g], at_x(-r)).wait_recv()
        copy(s_c.at[slot_ds(g)], r_c.at[slot_ds(g)], x_send.at[2, g], x_recv.at[2, g], at_x(r)).wait_recv()
        for j in slots(g):
            mine, col_of = entry(x, j)
            nb[j] = jnp.where(col_of == x, mine, jnp.where(col_of == ahead, r_b[j], r_c[j]))
        raw = nb[2 * a : 2 * b].astype(F32).reshape(count * TOK, ENC)
        mean_square = jnp.sum(raw * raw, axis=-1, keepdims=True) * (1.0 / ENC)
        normed = (raw * lax.rsqrt(mean_square + 1e-06)).astype(BF16)
        for t in range(TILES // 2):
            w2 = jnp.concatenate([wenc[2 * t], wenc[2 * t + 1]], axis=1)
            summed = jnp.dot(normed, w2, preferred_element_type=F32)
            width = min(256, ENC - 256 * t)
            summed = summed[:, :width]
            part = raw[:, 256 * t : 256 * t + width]
            enc[h, rows, 256 * t : 256 * t + width] = (part + summed * jax.nn.sigmoid(summed)).astype(BF16)
        gather = Gather(
            lambda t, rows=rows: enc.at[t, rows],
            lambda n, g=g: y_send.at[g, n],
            lambda n, g=g: y_recv.at[g, n],
            lambda n, g=g: y_sib.at[g, n],
        )
        gather.start()
        gathers.append(gather)

    locals_[2].wait()
    locals_[3].wait()

    def project(g, chip):
        a, b = GROUPS[g]
        n = 16 * (b - a)
        rows = pl.ds(16 * a, n)
        pair = pl.ds(2 * chip, 2)
        lhs = enc[pair, rows, :].reshape(2 * n, ENC)
        for w, out in ((wk, kbuf), (wv, vbuf)):
            got = jnp.dot(lhs, w[...], preferred_element_type=F32).astype(BF16)
            out[pair, rows, :] = got.reshape(2, n, COLS)

    for g in range(n_groups):
        gathers[g].from_sibling(0)
        project(g, y)
        gathers[g].arrive(0)
        gathers[g].arrive(1)
        for dy in (1, 3):
            gathers[g].from_sibling(dy)
            project(g, wrap(y + dy, NY))
        gathers[g].arrive(2)
        gathers[g].from_sibling(2)
        project(g, wrap(y + 2, NY))

    locals_[4].wait()
    for n, (dy, e) in enumerate(others):
        src = 2 * wrap(y + dy, NY) + wrap(c + e, NC)
        copy(qbuf.at[src], qbuf.at[src], q_send.at[n], q_recv.at[src], sibling).wait_recv()

    def attend(chunk):
        first = lax.div(11 * chunk, 8) - lax.div(chunk, 7)
        token = lax.broadcasted_iota(jnp.int32, (ROWS, 128), 0) + ROWS * chunk
        span_of = token >> 6
        for hd in range(COLS // HEAD_DIM):
            cols = slice(hd * HEAD_DIM, (hd + 1) * HEAD_DIM)

            def window(ref):
                spans = []
                for s in range(3):
                    rows = pl.ds(pl.multiple_of(16 * (first + s), 16), 16)
                    spans.append(ref[:, rows, cols].reshape(128, HEAD_DIM))
                return jnp.concatenate(spans, axis=0)

            scores = lax.dot_general(
                qbuf[chunk, :, cols], window(kbuf), (((1,), (1,)), ((), ())),
                preferred_element_type=F32,
            ) * HEAD_DIM ** (-0.5)
            parts = [
                jnp.where(span_of == first + s, scores[:, 128 * s : 128 * s + 128], -1e30) for s in range(3)
            ]
            highest = jnp.max(jnp.maximum(jnp.maximum(parts[0], parts[1]), parts[2]), axis=-1, keepdims=True)
            weights = [jnp.exp(p - highest) for p in parts]
            total = jnp.sum(weights[0] + weights[1] + weights[2], axis=-1, keepdims=True)
            probs = jnp.concatenate([(w / total).astype(BF16) for w in weights], axis=1)
            mixed = jnp.dot(probs, window(vbuf), preferred_element_type=F32)
            obuf[chunk, :, cols] = mixed.astype(BF16)

    for n, (dy, e) in enumerate(others[1:] + others[:1]):
        dev = at_head(dy, e)
        chunk = 2 * dev[2] + dev[3]
        attend(chunk)
        go(copy(obuf.at[chunk], out_ref.at[:, own_cols], o_send.at[n], o_recv.at[h], dev))
    attend(h)
    own_out = pltpu.make_async_copy(obuf.at[h], out_ref.at[:, own_cols], local.at[5])
    own_out.start()
    own_out.wait()
    for dy, e in others:
        src = 2 * wrap(y + dy, NY) + wrap(c + e, NC)
        cols = pl.ds(pl.multiple_of(src * COLS, COLS), COLS)
        dst = out_ref.at[:, cols]
        copy(obuf.at[h], dst, o_send.at[0], o_recv.at[src], sibling).wait_recv()

    for cp in sends:
        cp.wait_send()

    def z_sent(d, k):
        dev = at_z(r)
        piece = wz.at[x, z]
        copy(piece, piece, wz_send.at[d, k], wz_recv.at[d, k], dev).wait_send()
        for i in range(SUB):
            piece = zpiece(z, i)
            copy(piece, piece, z_send.at[d, k, i], z_recv.at[d, k, i], dev).wait_send()

    @pl.loop(1, hops[1])
    def _(k):
        for d in range(2):
            z_sent(d, k)

    z_sent(0, hops[0] - 1)


def per_device(queries, database_rows, w_encoder, w_key, w_value, neighbour_ids):
    z = lax.axis_index("z")
    table = lax.dynamic_index_in_dim(neighbour_ids.reshape(NX, NZ, SLOTS), z, 1, keepdims=False)
    padded = jnp.pad(w_encoder, ((0, 16 - WROWS), (0, 128 * TILES - ENC)))
    tiles = padded.reshape(16, TILES, 128).transpose(1, 0, 2)
    g = len(GROUPS)
    dma = pltpu.SemaphoreType.DMA
    slots = pltpu.VMEM((SLOTS, TOK, ENC), BF16)
    any_ = pl.BlockSpec(memory_space=pl.ANY)
    return pl.pallas_call(
        kernel,
        out_shape=jax.ShapeDtypeStruct(queries.shape, BF16),
        in_specs=[pl.BlockSpec(memory_space=pltpu.SMEM)] + [any_] * 5,
        out_specs=any_,
        scratch_shapes=[
            pltpu.VMEM((NZ * ENTRIES, TOK, ENC), BF16),
            pltpu.VMEM((NX, NZ, 16, 128), BF16),
            pltpu.VMEM((TILES, ENC, 128), BF16),
            pltpu.VMEM((ENC, COLS), BF16),
            pltpu.VMEM((ENC, COLS), BF16),
            pltpu.VMEM((CHUNKS, ROWS, COLS), BF16),
            slots, slots, slots, slots, slots, slots, slots,
            pltpu.VMEM((CHUNKS, SLOTS * TOK, ENC), BF16),
            pltpu.VMEM((CHUNKS, SLOTS * TOK, COLS), BF16),
            pltpu.VMEM((CHUNKS, SLOTS * TOK, COLS), BF16),
            pltpu.VMEM((CHUNKS, ROWS, COLS), BF16),
            dma((2, NZ // 2, SUB)), dma((2, NZ // 2, SUB)),
            dma((2, NZ // 2)), dma((2, NZ // 2)),
            dma((6,)),
            dma((7,)), dma((CHUNKS,)),
            dma((NX,)), dma((NX,)),
            dma((7,)), dma((3,)), dma((NY,)),
            dma((3, g)), dma((3, g)),
            dma((g, 7)), dma((g, 3)), dma((g, NY)),
            dma((7,)), dma((CHUNKS,)),
        ],
        compiler_params=pltpu.CompilerParams(
            collective_id=0, has_side_effects=True, vmem_limit_bytes=48 * 1024 * 1024
        ),
        name="exchange_attend",
    )(table, database_rows, tiles, queries, w_key, w_value)


def solution(mesh):
    torus = Mesh(mesh.devices.reshape(NX, NZ, NY, NC), SEQ_HEAD)
    in_specs = (
        P(SEQ_HEAD, None), P(SEQ, HEAD, None), P(SEQ, None), P(None, HEAD), P(None, HEAD), P(),
    )
    return jax.shard_map(
        per_device, mesh=torus, in_specs=in_specs, out_specs=P(SEQ_HEAD, None), check_vma=False
    )
```

```python
import jax
import jax.numpy as jnp
from jax import lax
from jax.experimental import pallas as pl
from jax.experimental.pallas import tpu as pltpu
from jax.sharding import Mesh
from jax.sharding import PartitionSpec as P

HEAD_DIM = 128
NX, NZ, NY, NC = 4, 16, 4, 2
SEQ = ("x", "z")
HEAD = ("y", "c")
SEQ_HEAD = ("x", "z", "y", "c")
MESH = pl.DeviceIdType.MESH
BF16 = jnp.bfloat16
F32 = jnp.float32

ENC = 896
ENTRIES = 8
TOK = 8
SLOTS = 22
CAP = 2
SUB = 4
WROWS = 14
COLS = 512
ROWS = 88
CHUNKS = 8
TILES = 8
LEAP = 4

GROUPS = ((0, 5), (5, 9), (9, 13), (13, 16))
READY = {1: 0, 3: 1, 5: 2, 7: 3}
PIECES = ((0, 6), (6, 11))


def order_of(d, way):
    return 2 * d - 1 + way


def kernel(
    ids_ref, db_ref, wsh_ref, q_ref, wk_ref, wv_ref, out_ref,
    vtab, inv_ref, own_ref, z0, z1, z2, z3, wz, wenc, wk, wv, qbuf, s_x, r_x, raw, enc, kbuf, vbuf, obuf,
    z_send, z_recv, wz_send, wz_recv, local, q_send, q_recv,
    wx_send, wx_recv, wy_send, wy_recv, wy_sib, x_send, x_recv,
    y_send, y_recv, e_send, e_recv, o_send, o_recv,
):
    x, z, y, c = (lax.axis_index(a) for a in SEQ_HEAD)
    r = 1 - 2 * c
    h = 2 * y + c
    zg = (z0, z1, z2, z3)

    def wrap(v, n):
        return lax.rem(v + 2 * n, n)

    def copy(src, dst, ssem, rsem, dev):
        return pltpu.make_async_remote_copy(
            src_ref=src, dst_ref=dst, send_sem=ssem, recv_sem=rsem,
            device_id=dev, device_id_type=MESH,
        )

    sibling = (x, z, y, 1 - c)

    def at_x(dx):
        return (wrap(x + dx, NX), z, y, c)

    def at_z(dz):
        return (x, wrap(z + dz, NZ), y, c)

    def at_y(dy):
        return (x, z, wrap(y + dy, NY), c)

    others = [(0, 1)] + [(dy, e) for dy in (2, 1, 3) for e in (0, 1)]

    def at_head(dy, e):
        return (x, z, wrap(y + dy, NY), wrap(c + e, NC))

    barrier = pltpu.get_barrier_semaphore()
    partners = [at_z(s * d) for d in range(1, LEAP + 1) for s in (1, -1)]
    partners += [at_x(n) for n in range(1, NX)] + [at_head(*o) for o in others]
    for dev in partners:
        pl.semaphore_signal(barrier, inc=1, device_id=dev, device_id_type=MESH)
    pl.semaphore_wait(barrier, len(partners))

    sends = []

    def go(cp):
        cp.start()
        sends.append(cp)

    def w_copy(n, slot, dist):
        return copy(wz.at[x, slot], wz.at[x, slot], wz_send.at[n], wz_recv.at[slot], at_z(r * dist))

    for n, d in enumerate([s * d for d in range(1, LEAP + 1) for s in (1, -1)]):
        slot = d % NZ
        go(copy(wsh_ref.at[h], wz.at[x, slot], wz_send.at[n], wz_recv.at[slot], at_z(r * d)))

    def zpiece(place, i):
        g = next(k for k, (a, b) in enumerate(GROUPS) if a <= place < b)
        n = ENTRIES // SUB
        return zg[g].at[pl.ds((place - GROUPS[g][0]) * ENTRIES + i * n, n)]

    def z_dev(way):
        return at_z(r if way == 0 else -r)

    for i in range(SUB):
        for way in range(2):
            go(copy(
                db_ref.at[pl.ds(i * (ENTRIES // SUB), ENTRIES // SUB)], zpiece(order_of(1, way), i),
                z_send.at[way, 0, i], z_recv.at[way, 0, i], z_dev(way),
            ))

    for n, (dy, e) in enumerate(others):
        dev = at_head(dy, e)
        to = 2 * dev[2] + dev[3]
        cols = pl.ds(pl.multiple_of(to * COLS, COLS), COLS)
        go(copy(q_ref.at[:, cols], qbuf.at[h], q_send.at[n], q_recv.at[h], dev))

    own_cols = pl.ds(pl.multiple_of(h * COLS, COLS), COLS)
    locals_ = [
        pltpu.make_async_copy(db_ref, z0.at[pl.ds(0, ENTRIES)], local.at[0]),
        pltpu.make_async_copy(wsh_ref.at[h], wz.at[x, 0], local.at[1]),
        pltpu.make_async_copy(wk_ref, wk, local.at[2]),
        pltpu.make_async_copy(wv_ref, wv, local.at[3]),
        pltpu.make_async_copy(q_ref.at[:, own_cols], qbuf.at[h], local.at[4]),
    ]
    for cp in locals_:
        cp.start()

    ids = ids_ref[...]
    lane = lax.broadcasted_iota(jnp.int32, (8, 128), 1)
    owner_of = ids >> 3
    number = jnp.zeros_like(ids)
    for k in range(1, SLOTS):
        same = (pltpu.roll(owner_of, k, 1) == owner_of) & (lane >= k)
        number = number + jnp.where(same, 1, 0)
    behind = (r * (z - (owner_of & (NZ - 1)))) & (NZ - 1)
    place_of = jnp.where(behind < NZ // 2, jnp.maximum(2 * behind - 1, 0), 2 * (NZ - behind))
    place_of = jnp.where(behind == NZ // 2, NZ - 1, place_of)
    slot_of = CAP * place_of + number
    column_of = owner_of >> 4
    key = jnp.where(column_of == x, slot_of * ENTRIES + (ids & (ENTRIES - 1)), -1)
    inverse = jnp.zeros_like(ids)
    for k in range(SLOTS):
        one = jnp.broadcast_to(key[:, k : k + 1], (8, 128))
        inverse = inverse + jnp.where((one >> 3) == lane, one & (ENTRIES - 1), 0)
    vtab[0] = inverse
    vtab[1] = slot_of * NX + column_of
    to_scalar = [
        pltpu.make_async_copy(vtab.at[0], inv_ref, local.at[6]),
        pltpu.make_async_copy(vtab.at[1], own_ref, local.at[7]),
    ]
    for cp in to_scalar:
        cp.start()

    def z_step(k):
        d = k + 1
        for i in range(SUB):
            for way in range(2):
                if d == NZ // 2 and way == 1:
                    continue
                piece = zpiece(order_of(d, way), i)
                copy(piece, piece, z_send.at[way, k, i], z_recv.at[way, k, i], z_dev(way)).wait_recv()
                if d + 1 < NZ // 2 or (d + 1 == NZ // 2 and way == 0):
                    go(copy(
                        piece, zpiece(order_of(d + 1, way), i),
                        z_send.at[way, k + 1, i], z_recv.at[way, k + 1, i], z_dev(way),
                    ))

    def w_arrived(slot):
        copy(wz.at[x, slot], wz.at[x, slot], wz_send.at[0], wz_recv.at[slot], at_z(1)).wait_recv()

    def w_leap():
        n = 2 * LEAP
        for s in (1, -1):
            held = s * LEAP % NZ
            w_arrived(held)
            for d in range(1, LEAP + 1):
                total = LEAP + d
                if total == NZ // 2 and s == -1:
                    continue
                slot = s * total % NZ
                go(copy(wz.at[x, held], wz.at[x, slot], wz_send.at[n], wz_recv.at[slot], at_z(s * r * d)))
                n += 1

    def w_columns():
        for slot in range(1, NZ):
            if slot not in (LEAP, NZ - LEAP):
                w_arrived(slot)
        locals_[1].wait()
        for n in range(1, NX):
            go(copy(wz.at[x], wz.at[x], wx_send.at[n], wx_recv.at[x], at_x(n)))

    class Gather:
        def start(self):
            own = wenc.at[h]
            go(copy(own, own, wy_send.at[0], wy_recv.at[0], at_y(r)))
            go(copy(own, own, wy_send.at[1], wy_recv.at[1], at_y(-r)))
            go(copy(own, own, wy_send.at[2], wy_sib.at[0], sibling))

        def arrive(self, n):
            step = (-1, 1, 2)[n] * r
            piece = wenc.at[2 * wrap(y + step, NY) + c]
            copy(piece, piece, wy_send.at[0], wy_recv.at[n], at_y(r)).wait_recv()
            if n == 0:
                go(copy(piece, piece, wy_send.at[3], wy_recv.at[2], at_y(r)))
            go(copy(piece, piece, wy_send.at[4 + n], wy_sib.at[wrap(step, NY)], sibling))

        def from_sibling(self, delta):
            piece = wenc.at[2 * wrap(y + delta, NY) + 1 - c]
            copy(piece, piece, wy_send.at[0], wy_sib.at[delta], sibling).wait_recv()

    w_gather = Gather()

    def w_pack():
        for n in range(1, NX):
            src = wrap(x + n, NX)
            copy(wz.at[src], wz.at[src], wx_send.at[n], wx_recv.at[src], at_x(n)).wait_recv()
        lhs_rows, rhs_rows = ENTRIES * WROWS, NZ * 16
        row = lax.broadcasted_iota(jnp.int32, (lhs_rows, rhs_rows), 0)
        col = lax.broadcasted_iota(jnp.int32, (lhs_rows, rhs_rows), 1)
        owner = (z - r * (col >> 4)) & (NZ - 1)
        inner = col & 15
        place = owner * WROWS + inner
        for b in range(2):
            pick = jnp.where((inner < WROWS) & (place == row + b * lhs_rows), 1.0, 0.0).astype(BF16)
            for a in range(NX):
                block = wz[a].reshape(rhs_rows, 128)
                packed = jnp.dot(pick, block, preferred_element_type=F32).astype(BF16)
                wenc[h, pl.ds((2 * a + b) * lhs_rows, lhs_rows), :] = packed
        w_gather.start()

    def x_slots(g):
        return CAP * GROUPS[g][0], CAP * (GROUPS[g][1] - GROUPS[g][0])

    def x_exchange(g):
        first, count = x_slots(g)
        for n in (2, 1, 3, 0):
            dest = wrap(x + n, NX)
            for j in range(first, first + count):
                at = (j // CAP - GROUPS[g][0]) * ENTRIES + (inv_ref[dest, j] & (ENTRIES - 1))
                if n:
                    s_x[n - 1, j] = zg[g][at]
                else:
                    r_x[x, j] = zg[g][at]
            if n:
                part = pl.ds(first, count)
                go(copy(s_x.at[n - 1, part], r_x.at[x, part], x_send.at[n, g], x_recv.at[x, g], at_x(n)))

    locals_[0].wait()
    for cp in to_scalar:
        cp.wait()
    for k in range(NZ // 2):
        z_step(k)
        if k == 0:
            w_leap()
        if k in READY:
            x_exchange(READY[k])
        if k == 2:
            w_columns()
        if k == 4:
            w_pack()
        if k == 6:
            w_gather.arrive(0)
            w_gather.arrive(1)

    for g in range(len(GROUPS)):
        first, count = x_slots(g)
        for n in range(1, NX):
            src = wrap(x + n, NX)
            part = r_x.at[src, pl.ds(first, count)]
            copy(part, part, x_send.at[n, g], x_recv.at[src, g], at_x(n)).wait_recv()

    def slots_of(p):
        a, b = PIECES[p]
        return pl.ds(2 * a, 2 * (b - a))

    def y_part(step, p):
        return raw.at[wrap(y + step, NY), slots_of(p)]

    for p, (a, b) in enumerate(PIECES):
        for j in range(2 * a, 2 * b):
            code = own_ref[x, (j % 2) * (SLOTS // 2) + j // 2]
            raw[y, j] = r_x[code & (NX - 1), (code >> 2) & (CAP * NZ - 1)]
        own = y_part(0, p)
        go(copy(own, own, y_send.at[0, p], y_recv.at[0, p], at_y(r)))
        go(copy(own, own, y_send.at[1, p], y_recv.at[1, p], at_y(-r)))

    w_gather.arrive(2)
    for n in range(NY):
        w_gather.from_sibling(n)

    def y_arrive(n, p):
        piece = y_part((-1, 1, 2)[n] * r, p)
        copy(piece, piece, y_send.at[0, p], y_recv.at[n, p], at_y(r)).wait_recv()
        if n == 0:
            go(copy(piece, piece, y_send.at[2, p], y_recv.at[2, p], at_y(r)))

    def rows_of(p):
        a, b = PIECES[p]
        return pl.ds(16 * a, 16 * (b - a)), 16 * (b - a)

    def encode(step, p):
        chip = wrap(y + step, NY)
        rows, count = rows_of(p)
        here = 2 * chip + c
        rawf = raw[chip, slots_of(p)].astype(F32).reshape(count, ENC)
        mean_square = jnp.sum(rawf * rawf, axis=-1, keepdims=True) * (1.0 / ENC)
        normed = (rawf * lax.rsqrt(mean_square + 1e-06)).astype(BF16)
        for t in range(TILES // 2):
            w2 = jnp.concatenate([wenc[2 * t], wenc[2 * t + 1]], axis=1)
            summed = jnp.dot(normed, w2, preferred_element_type=F32)
            width = min(256, ENC - 256 * t)
            summed = summed[:, :width]
            part = rawf[:, 256 * t : 256 * t + width]
            enc[here, rows, 256 * t : 256 * t + width] = (part + summed * jax.nn.sigmoid(summed)).astype(BF16)
        own = enc.at[here, rows]
        delta = wrap(step, NY)
        go(copy(own, own, e_send.at[delta, p], e_recv.at[delta, p], sibling))

    def project(step, p):
        chip = wrap(y + step, NY)
        rows, n = rows_of(p)
        theirs = enc.at[2 * chip + 1 - c, rows]
        delta = wrap(step, NY)
        copy(theirs, theirs, e_send.at[delta, p], e_recv.at[delta, p], sibling).wait_recv()
        pair = pl.ds(2 * chip, 2)
        lhs = enc[pair, rows, :].reshape(2 * n, ENC)
        for w, out in ((wk, kbuf), (wv, vbuf)):
            got = jnp.dot(lhs, w[...], preferred_element_type=F32).astype(BF16)
            out[pair, rows, :] = got.reshape(2, n, COLS)

    def attend(chunk):
        first = chunk + lax.div(chunk, 5)
        token = lax.broadcasted_iota(jnp.int32, (ROWS, 128), 0) + ROWS * chunk
        span_of = token >> 6
        for hd in range(COLS // HEAD_DIM):
            cols = slice(hd * HEAD_DIM, (hd + 1) * HEAD_DIM)

            def window(ref):
                spans = []
                for s in range(3):
                    rows = pl.ds(pl.multiple_of(16 * (first + s), 16), 16)
                    spans.append(ref[:, rows, cols].reshape(128, HEAD_DIM))
                return jnp.concatenate(spans, axis=0)

            scores = lax.dot_general(
                qbuf[chunk, :, cols], window(kbuf), (((1,), (1,)), ((), ())),
                preferred_element_type=F32,
            ) * HEAD_DIM ** (-0.5)
            parts = [
                jnp.where(span_of == first + s, scores[:, 128 * s : 128 * s + 128], -1e30) for s in range(3)
            ]
            highest = jnp.max(jnp.maximum(jnp.maximum(parts[0], parts[1]), parts[2]), axis=-1, keepdims=True)
            weights = [jnp.exp(p - highest) for p in parts]
            total = jnp.sum(weights[0] + weights[1] + weights[2], axis=-1, keepdims=True)
            probs = jnp.concatenate([(w / total).astype(BF16) for w in weights], axis=1)
            mixed = jnp.dot(probs, window(vbuf), preferred_element_type=F32)
            obuf[chunk, :, cols] = mixed.astype(BF16)

    def out_copy(chunk):
        dev = (x, z, lax.div(chunk, NC), lax.rem(chunk, NC))
        return copy(obuf.at[chunk], out_ref.at[:, own_cols], o_send.at[chunk], o_recv.at[h], dev)

    own_out = pltpu.make_async_copy(obuf.at[h], out_ref.at[:, own_cols], local.at[5])

    encode(0, 0)
    y_arrive(0, 0)
    encode(0, 1)
    y_arrive(0, 1)
    locals_[2].wait()
    locals_[3].wait()
    for p in range(2):
        encode(-r, p)
        y_arrive(1, p)
        encode(r, p)
        project(0, p)
        for step in (1, -1):
            project(step, p)
        y_arrive(2, p)
        encode(2, p)
        project(2, p)
        if p == 0:
            locals_[4].wait()
            for n, (dy, e) in enumerate(others):
                src = 2 * wrap(y + dy, NY) + wrap(c + e, NC)
                copy(qbuf.at[src], qbuf.at[src], q_send.at[n], q_recv.at[src], sibling).wait_recv()

        @pl.loop(p * CHUNKS // 2, (p + 1) * CHUNKS // 2)
        def _(chunk):
            attend(chunk)

            @pl.when(chunk == h)
            def _():
                own_out.start()

            @pl.when(chunk != h)
            def _():
                out_copy(chunk).start()

    own_out.wait()
    for dy, e in others:
        src = 2 * wrap(y + dy, NY) + wrap(c + e, NC)
        cols = pl.ds(pl.multiple_of(src * COLS, COLS), COLS)
        copy(obuf.at[h], out_ref.at[:, cols], o_send.at[src], o_recv.at[src], sibling).wait_recv()
    for cp in sends:
        cp.wait_send()
    for dy, e in others:
        out_copy(2 * wrap(y + dy, NY) + wrap(c + e, NC)).wait_send()


def cited(neighbour_ids):
    ids = neighbour_ids.T.reshape(CAP, NX, NZ, SLOTS // 2)
    ids = lax.dynamic_index_in_dim(ids, lax.axis_index("z"), 2, keepdims=False)
    rows = jnp.concatenate([ids[0], ids[1]], axis=1)
    return jnp.pad(rows, ((0, 8 - NX), (0, 128 - SLOTS)))


def per_device(queries, database_rows, w_encoder, w_key, w_value, neighbour_ids):
    padded = jnp.pad(w_encoder, ((0, 16 - WROWS), (0, 128 * TILES - ENC)))
    tiles = padded.reshape(16, TILES, 128).transpose(1, 0, 2)
    g, p = len(GROUPS), len(PIECES)
    dma = pltpu.SemaphoreType.DMA
    any_ = pl.BlockSpec(memory_space=pl.ANY)
    return pl.pallas_call(
        kernel,
        out_shape=jax.ShapeDtypeStruct(queries.shape, BF16),
        in_specs=[pl.BlockSpec(memory_space=pltpu.VMEM)] + [any_] * 5,
        out_specs=any_,
        scratch_shapes=[
            pltpu.VMEM((2, 8, 128), jnp.int32), pltpu.SMEM((8, 128), jnp.int32), pltpu.SMEM((8, 128), jnp.int32),
        ] + [pltpu.VMEM(((b - a) * ENTRIES, TOK, ENC), BF16) for a, b in GROUPS] + [
            pltpu.VMEM((NX, NZ, 16, 128), BF16),
            pltpu.VMEM((TILES, ENC, 128), BF16),
            pltpu.VMEM((ENC, COLS), BF16),
            pltpu.VMEM((ENC, COLS), BF16),
            pltpu.VMEM((CHUNKS, ROWS, COLS), BF16),
            pltpu.VMEM((NX - 1, CAP * NZ, TOK, ENC), BF16),
            pltpu.VMEM((NX, CAP * NZ, TOK, ENC), BF16),
            pltpu.VMEM((NY, SLOTS, TOK, ENC), BF16),
            pltpu.VMEM((CHUNKS, SLOTS * TOK, ENC), BF16),
            pltpu.VMEM((CHUNKS, SLOTS * TOK, COLS), BF16),
            pltpu.VMEM((CHUNKS, SLOTS * TOK, COLS), BF16),
            pltpu.VMEM((CHUNKS, ROWS, COLS), BF16),
            dma((2, NZ // 2, SUB)), dma((2, NZ // 2, SUB)),
            dma((NZ,)), dma((NZ,)),
            dma((8,)),
            dma((7,)), dma((CHUNKS,)),
            dma((NX,)), dma((NX,)),
            dma((7,)), dma((3,)), dma((NY,)),
            dma((NX, g)), dma((NX, g)),
            dma((3, p)), dma((3, p)),
            dma((NY, p)), dma((NY, p)),
            dma((CHUNKS,)), dma((CHUNKS,)),
        ],
        compiler_params=pltpu.CompilerParams(collective_id=0, has_side_effects=True),
        name="exchange_attend",
    )(cited(neighbour_ids), database_rows, tiles, queries, w_key, w_value)


def solution(mesh):
    torus = Mesh(mesh.devices.reshape(NX, NZ, NY, NC), SEQ_HEAD)
    in_specs = (
        P(SEQ_HEAD, None), P(SEQ, HEAD, None), P(SEQ, None), P(None, HEAD), P(None, HEAD), P(),
    )
    return jax.shard_map(
        per_device, mesh=torus, in_specs=in_specs, out_specs=P(SEQ_HEAD, None), check_vma=False
    )
```

```python
import jax
import jax.numpy as jnp
from jax import lax
from jax.experimental import pallas as pl
from jax.experimental.pallas import tpu as pltpu
from jax.sharding import Mesh
from jax.sharding import PartitionSpec as P

HEAD_DIM = 128
NX, NZ, NY, NC = 4, 16, 4, 2
SEQ = ("x", "z")
HEAD = ("y", "c")
SEQ_HEAD = ("x", "z", "y", "c")
MESH = pl.DeviceIdType.MESH
BF16 = jnp.bfloat16
F32 = jnp.float32

ENC = 896
ENTRIES = 8
TOK = 8
SLOTS = 22
CAP = 2
SUB = 4
WROWS = 14
COLS = 512
ROWS = 88
CHUNKS = 8
TILES = 8
LEAP = 4

GROUPS = ((0, 5), (5, 9), (9, 13), (13, 16))
READY = {1: 0, 3: 1, 5: 2, 7: 3}

SPAN = 64
SPANS = (0, 1, 4, 5, 6, 9, 10, 2, 3, 7, 8)
PIECES = ((0, 7), (7, 11))
HALVES = ((0, 3, 4, 7), (1, 2, 5, 6))


def order_of(d, way):
    return 2 * d - 1 + way


def kernel(
    ids_hbm, db_ref, wsh_ref, q_ref, wk_ref, wv_ref, out_ref,
    ids_ref, vtab, inv_ref, own_ref, z0, z1, z2, z3, wz, wenc, wk, wv, qbuf, s_x, r_x, raw, enc, kbuf, vbuf, mixed, obuf,
    z_send, z_recv, wz_send, wz_recv, local, q_send, q_recv,
    wx_send, wx_recv, wy_send, wy_recv, wy_sib, x_send, x_recv,
    y_send, y_recv, e_send, e_recv, o_send, o_recv,
):
    x, z, y, c = (lax.axis_index(a) for a in SEQ_HEAD)
    r = 1 - 2 * c
    h = 2 * y + c
    zg = (z0, z1, z2, z3)

    def wrap(v, n):
        return lax.rem(v + 2 * n, n)

    def copy(src, dst, ssem, rsem, dev):
        return pltpu.make_async_remote_copy(
            src_ref=src, dst_ref=dst, send_sem=ssem, recv_sem=rsem,
            device_id=dev, device_id_type=MESH,
        )

    sibling = (x, z, y, 1 - c)

    def at_x(dx):
        return (wrap(x + dx, NX), z, y, c)

    def at_z(dz):
        return (x, wrap(z + dz, NZ), y, c)

    def at_y(dy):
        return (x, z, wrap(y + dy, NY), c)

    others = [(0, 1)] + [(dy, e) for dy in (2, 1, 3) for e in (0, 1)]

    def at_head(dy, e):
        return (x, z, wrap(y + dy, NY), wrap(c + e, NC))

    read_ids = pltpu.make_async_copy(ids_hbm, ids_ref, local.at[8])
    read_ids.start()

    barrier = pltpu.get_barrier_semaphore()
    partners = [at_z(s * d) for d in range(1, LEAP + 1) for s in (1, -1)]
    partners += [at_x(n) for n in range(1, NX)] + [at_head(*o) for o in others]
    for dev in partners:
        pl.semaphore_signal(barrier, inc=1, device_id=dev, device_id_type=MESH)
    pl.semaphore_wait(barrier, len(partners))

    sends = []

    def go(cp):
        cp.start()
        sends.append(cp)

    def w_copy(n, slot, dist):
        return copy(wz.at[x, slot], wz.at[x, slot], wz_send.at[n], wz_recv.at[slot], at_z(r * dist))

    for n, d in enumerate([s * d for d in range(1, LEAP + 1) for s in (1, -1)]):
        slot = d % NZ
        go(copy(wsh_ref.at[h], wz.at[x, slot], wz_send.at[n], wz_recv.at[slot], at_z(r * d)))

    def zpiece(place, i):
        g = next(k for k, (a, b) in enumerate(GROUPS) if a <= place < b)
        n = ENTRIES // SUB
        return zg[g].at[pl.ds((place - GROUPS[g][0]) * ENTRIES + i * n, n)]

    def z_dev(way):
        return at_z(r if way == 0 else -r)

    for i in range(SUB):
        for way in range(2):
            go(copy(
                db_ref.at[pl.ds(i * (ENTRIES // SUB), ENTRIES // SUB)], zpiece(order_of(1, way), i),
                z_send.at[way, 0, i], z_recv.at[way, 0, i], z_dev(way),
            ))

    for n, (dy, e) in enumerate(others):
        dev = at_head(dy, e)
        to = 2 * dev[2] + dev[3]
        cols = pl.ds(pl.multiple_of(to * COLS, COLS), COLS)
        go(copy(q_ref.at[:, cols], qbuf.at[h], q_send.at[n], q_recv.at[h], dev))

    own_cols = pl.ds(pl.multiple_of(h * COLS, COLS), COLS)
    locals_ = [
        pltpu.make_async_copy(db_ref, z0.at[pl.ds(0, ENTRIES)], local.at[0]),
        pltpu.make_async_copy(wsh_ref.at[h], wz.at[x, 0], local.at[1]),
        pltpu.make_async_copy(wk_ref, wk, local.at[2]),
        pltpu.make_async_copy(wv_ref, wv, local.at[3]),
        pltpu.make_async_copy(q_ref.at[:, own_cols], qbuf.at[h], local.at[4]),
    ]
    for cp in locals_:
        cp.start()

    read_ids.wait()
    ids = ids_ref[...]
    lane = lax.broadcasted_iota(jnp.int32, (8, 128), 1)
    owner_of = ids >> 3
    number = jnp.zeros_like(ids)
    for k in range(1, SLOTS):
        same = (pltpu.roll(owner_of, k, 1) == owner_of) & (lane >= k)
        number = number + jnp.where(same, 1, 0)
    behind = (r * (z - (owner_of & (NZ - 1)))) & (NZ - 1)
    place_of = jnp.where(behind < NZ // 2, jnp.maximum(2 * behind - 1, 0), 2 * (NZ - behind))
    place_of = jnp.where(behind == NZ // 2, NZ - 1, place_of)
    slot_of = CAP * place_of + number
    column_of = owner_of >> 4
    key = jnp.where(column_of == x, slot_of * ENTRIES + (ids & (ENTRIES - 1)), -1)
    inverse = jnp.zeros_like(ids)
    for k in range(SLOTS):
        one = jnp.broadcast_to(key[:, k : k + 1], (8, 128))
        inverse = inverse + jnp.where((one >> 3) == lane, one & (ENTRIES - 1), 0)
    vtab[0] = inverse
    vtab[1] = slot_of * NX + column_of
    to_scalar = [
        pltpu.make_async_copy(vtab.at[0], inv_ref, local.at[6]),
        pltpu.make_async_copy(vtab.at[1], own_ref, local.at[7]),
    ]
    for cp in to_scalar:
        cp.start()

    def z_step(k):
        d = k + 1
        for i in range(SUB):
            for way in range(2):
                if d == NZ // 2 and way == 1:
                    continue
                piece = zpiece(order_of(d, way), i)
                copy(piece, piece, z_send.at[way, k, i], z_recv.at[way, k, i], z_dev(way)).wait_recv()
                if d + 1 < NZ // 2 or (d + 1 == NZ // 2 and way == 0):
                    go(copy(
                        piece, zpiece(order_of(d + 1, way), i),
                        z_send.at[way, k + 1, i], z_recv.at[way, k + 1, i], z_dev(way),
                    ))

    def w_arrived(slot):
        copy(wz.at[x, slot], wz.at[x, slot], wz_send.at[0], wz_recv.at[slot], at_z(1)).wait_recv()

    def w_leap():
        n = 2 * LEAP
        for s in (1, -1):
            held = s * LEAP % NZ
            w_arrived(held)
            for d in range(1, LEAP + 1):
                total = LEAP + d
                if total == NZ // 2 and s == -1:
                    continue
                slot = s * total % NZ
                go(copy(wz.at[x, held], wz.at[x, slot], wz_send.at[n], wz_recv.at[slot], at_z(s * r * d)))
                n += 1

    def w_columns():
        for slot in range(1, NZ):
            if slot not in (LEAP, NZ - LEAP):
                w_arrived(slot)
        locals_[1].wait()
        for n in range(1, NX):
            go(copy(wz.at[x], wz.at[x], wx_send.at[n], wx_recv.at[x], at_x(n)))

    class Gather:
        def start(self):
            own = wenc.at[h]
            go(copy(own, own, wy_send.at[0], wy_recv.at[0], at_y(r)))
            go(copy(own, own, wy_send.at[1], wy_recv.at[1], at_y(-r)))
            go(copy(own, own, wy_send.at[2], wy_sib.at[0], sibling))

        def arrive(self, n):
            step = (-1, 1, 2)[n] * r
            piece = wenc.at[2 * wrap(y + step, NY) + c]
            copy(piece, piece, wy_send.at[0], wy_recv.at[n], at_y(r)).wait_recv()
            if n == 0:
                go(copy(piece, piece, wy_send.at[3], wy_recv.at[2], at_y(r)))
            go(copy(piece, piece, wy_send.at[4 + n], wy_sib.at[wrap(step, NY)], sibling))

        def from_sibling(self, delta):
            piece = wenc.at[2 * wrap(y + delta, NY) + 1 - c]
            copy(piece, piece, wy_send.at[0], wy_sib.at[delta], sibling).wait_recv()

    w_gather = Gather()

    def w_pack():
        for n in range(1, NX):
            src = wrap(x + n, NX)
            copy(wz.at[src], wz.at[src], wx_send.at[n], wx_recv.at[src], at_x(n)).wait_recv()
        lhs_rows, rhs_rows = ENTRIES * WROWS, NZ * 16
        row = lax.broadcasted_iota(jnp.int32, (lhs_rows, rhs_rows), 0)
        col = lax.broadcasted_iota(jnp.int32, (lhs_rows, rhs_rows), 1)
        owner = (z - r * (col >> 4)) & (NZ - 1)
        inner = col & 15
        place = owner * WROWS + inner
        for b in range(2):
            pick = jnp.where((inner < WROWS) & (place == row + b * lhs_rows), 1.0, 0.0).astype(BF16)
            for a in range(NX):
                block = wz[a].reshape(rhs_rows, 128)
                packed = jnp.dot(pick, block, preferred_element_type=F32).astype(BF16)
                wenc[h, pl.ds((2 * a + b) * lhs_rows, lhs_rows), :] = packed
        w_gather.start()

    def x_slots(g):
        return CAP * GROUPS[g][0], CAP * (GROUPS[g][1] - GROUPS[g][0])

    def x_exchange(g):
        first, count = x_slots(g)
        for n in (2, 1, 3, 0):
            dest = wrap(x + n, NX)
            for j in range(first, first + count):
                at = (j // CAP - GROUPS[g][0]) * ENTRIES + (inv_ref[dest, j] & (ENTRIES - 1))
                if n:
                    s_x[n - 1, j] = zg[g][at]
                else:
                    r_x[x, j] = zg[g][at]
            if n:
                part = pl.ds(first, count)
                go(copy(s_x.at[n - 1, part], r_x.at[x, part], x_send.at[n, g], x_recv.at[x, g], at_x(n)))

    locals_[0].wait()
    for cp in to_scalar:
        cp.wait()
    for k in range(NZ // 2):
        z_step(k)
        if k == 0:
            w_leap()
        if k in READY:
            x_exchange(READY[k])
        if k == 2:
            w_columns()
        if k == 4:
            w_pack()
        if k == 6:
            w_gather.arrive(0)
            w_gather.arrive(1)

    for g in range(len(GROUPS)):
        first, count = x_slots(g)
        for n in range(1, NX):
            src = wrap(x + n, NX)
            part = r_x.at[src, pl.ds(first, count)]
            copy(part, part, x_send.at[n, g], x_recv.at[src, g], at_x(n)).wait_recv()

    def slots_of(p):
        a, b = PIECES[p]
        return pl.ds(2 * a, 2 * (b - a))

    def y_part(step, p):
        return raw.at[wrap(y + step, NY), slots_of(p)]

    for p, (a, b) in enumerate(PIECES):
        for j in range(2 * a, 2 * b):
            code = own_ref[x, (j % 2) * (SLOTS // 2) + SPANS[j // 2]]
            raw[y, j] = r_x[code & (NX - 1), (code >> 2) & (CAP * NZ - 1)]
        own = y_part(0, p)
        go(copy(own, own, y_send.at[0, p], y_recv.at[0, p], at_y(r)))
        go(copy(own, own, y_send.at[1, p], y_recv.at[1, p], at_y(-r)))

    w_gather.arrive(2)
    for n in range(NY):
        w_gather.from_sibling(n)

    def y_arrive(n, p):
        piece = y_part((-1, 1, 2)[n] * r, p)
        copy(piece, piece, y_send.at[0, p], y_recv.at[n, p], at_y(r)).wait_recv()
        if n == 0:
            go(copy(piece, piece, y_send.at[2, p], y_recv.at[2, p], at_y(r)))

    def rows_of(p):
        a, b = PIECES[p]
        return pl.ds(16 * a, 16 * (b - a)), 16 * (b - a)

    def encode(step, p):
        chip = wrap(y + step, NY)
        rows, count = rows_of(p)
        here = 2 * chip + c
        rawf = raw[chip, slots_of(p)].astype(F32).reshape(count, ENC)
        mean_square = jnp.sum(rawf * rawf, axis=-1, keepdims=True) * (1.0 / ENC)
        normed = (rawf * lax.rsqrt(mean_square + 1e-06)).astype(BF16)
        for t in range(TILES // 2):
            w2 = jnp.concatenate([wenc[2 * t], wenc[2 * t + 1]], axis=1)
            summed = jnp.dot(normed, w2, preferred_element_type=F32)
            width = min(256, ENC - 256 * t)
            summed = summed[:, :width]
            part = rawf[:, 256 * t : 256 * t + width]
            enc[here, rows, 256 * t : 256 * t + width] = (part + summed * jax.nn.sigmoid(summed)).astype(BF16)
        own = enc.at[here, rows]
        delta = wrap(step, NY)
        go(copy(own, own, e_send.at[delta, p], e_recv.at[delta, p], sibling))

    def project(step, p):
        chip = wrap(y + step, NY)
        rows, n = rows_of(p)
        theirs = enc.at[2 * chip + 1 - c, rows]
        delta = wrap(step, NY)
        copy(theirs, theirs, e_send.at[delta, p], e_recv.at[delta, p], sibling).wait_recv()
        pair = pl.ds(2 * chip, 2)
        lhs = enc[pair, rows, :].reshape(2 * n, ENC)
        for w, out in ((wk, kbuf), (wv, vbuf)):
            got = jnp.dot(lhs, w[...], preferred_element_type=F32).astype(BF16)
            out[pair, rows, :] = got.reshape(2, n, COLS)

    def attend(spans):
        heads = [slice(hd * HEAD_DIM, (hd + 1) * HEAD_DIM) for hd in range(COLS // HEAD_DIM)]
        pairs = [(span, cols) for span in spans for cols in heads]
        scores = []
        for span, cols in pairs:
            first, last = SPAN * span, SPAN * (span + 1)
            rows = []
            for chunk in range(first // ROWS, (last - 1) // ROWS + 1):
                a, b = max(first - ROWS * chunk, 0), min(last - ROWS * chunk, ROWS)
                rows.append(qbuf[chunk, :, cols].astype(F32)[a:b])
            q = jnp.concatenate(rows, axis=0).astype(BF16)
            at = 16 * SPANS.index(span)
            k = kbuf[:, at : at + 16, cols].reshape(128, HEAD_DIM)
            scores.append(lax.dot_general(q, k, (((1,), (1,)), ((), ())), preferred_element_type=F32))
        scores = jnp.concatenate(scores, axis=0) * HEAD_DIM ** (-0.5)
        weights = jnp.exp(scores - jnp.max(scores, axis=-1, keepdims=True))
        scale = 1.0 / jnp.sum(weights, axis=-1, keepdims=True)
        probs = (weights * scale).astype(BF16)
        outs = []
        for n, (span, cols) in enumerate(pairs):
            at = 16 * SPANS.index(span)
            v = vbuf[:, at : at + 16, cols].reshape(128, HEAD_DIM)
            outs.append(jnp.dot(probs[SPAN * n : SPAN * (n + 1)], v, preferred_element_type=F32))
        for out, (span, cols) in zip(outs, pairs):
            mixed[span, :, cols] = out

    def finish(chunk):
        first, last = ROWS * chunk, ROWS * (chunk + 1)
        rows = []
        for span in range(first // SPAN, (last - 1) // SPAN + 1):
            a, b = max(first - SPAN * span, 0), min(last - SPAN * span, SPAN)
            rows.append(mixed[span, a:b, :])
        obuf[chunk] = jnp.concatenate(rows, axis=0).astype(BF16)

        @pl.when(h == chunk)
        def _():
            own_out.start()

        @pl.when(h != chunk)
        def _():
            out_copy(chunk).start()

    def out_copy(chunk):
        dev = (x, z, chunk // NC, chunk % NC)
        return copy(obuf.at[chunk], out_ref.at[:, own_cols], o_send.at[chunk], o_recv.at[h], dev)

    own_out = pltpu.make_async_copy(obuf.at[h], out_ref.at[:, own_cols], local.at[5])

    encode(0, 0)
    y_arrive(0, 0)
    encode(0, 1)
    y_arrive(0, 1)
    locals_[2].wait()
    locals_[3].wait()
    for p in range(2):
        encode(-r, p)
        y_arrive(1, p)
        encode(r, p)
    for step, p in ((0, 0), (r, 0), (-r, 0), (0, 1)):
        project(step, p)
    locals_[4].wait()
    for n, (dy, e) in enumerate(others):
        src = 2 * wrap(y + dy, NY) + wrap(c + e, NC)
        copy(qbuf.at[src], qbuf.at[src], q_send.at[n], q_recv.at[src], sibling).wait_recv()
    y_arrive(2, 0)
    encode(2, 0)
    for step, p in ((r, 1), (-r, 1), (2, 0)):
        project(step, p)
    for chunks, spans in zip(HALVES[0], ((0, 1), (4, 5), (6,), (9, 10))):
        attend(spans)
        finish(chunks)
        if chunks == HALVES[0][1]:
            y_arrive(2, 1)
            encode(2, 1)
    project(2, 1)
    attend((2, 3))
    finish(1)
    finish(2)
    attend((7, 8))
    finish(5)
    finish(6)

    own_out.wait()
    for dy, e in others:
        src = 2 * wrap(y + dy, NY) + wrap(c + e, NC)
        cols = pl.ds(pl.multiple_of(src * COLS, COLS), COLS)
        copy(obuf.at[h], out_ref.at[:, cols], o_send.at[src], o_recv.at[src], sibling).wait_recv()
    for cp in sends:
        cp.wait_send()
    for dy, e in others:
        copy(obuf.at[h], obuf.at[h], o_send.at[2 * wrap(y + dy, NY) + wrap(c + e, NC)], o_recv.at[h], sibling).wait_send()


def cited(neighbour_ids):
    ids = neighbour_ids.T.reshape(CAP, NX, NZ, SLOTS // 2)
    ids = lax.dynamic_index_in_dim(ids, lax.axis_index("z"), 2, keepdims=False)
    rows = jnp.concatenate([ids[0], ids[1]], axis=1)
    return jnp.pad(rows, ((0, 8 - NX), (0, 128 - SLOTS)))


def per_device(queries, database_rows, w_encoder, w_key, w_value, neighbour_ids):
    padded = jnp.pad(w_encoder, ((0, 16 - WROWS), (0, 128 * TILES - ENC)))
    tiles = padded.reshape(16, TILES, 128).transpose(1, 0, 2)
    g, p = len(GROUPS), len(PIECES)
    dma = pltpu.SemaphoreType.DMA
    any_ = pl.BlockSpec(memory_space=pl.ANY)
    return pl.pallas_call(
        kernel,
        out_shape=jax.ShapeDtypeStruct(queries.shape, BF16),
        in_specs=[any_] * 6,
        out_specs=any_,
        scratch_shapes=[
            pltpu.VMEM((8, 128), jnp.int32),
            pltpu.VMEM((2, 8, 128), jnp.int32), pltpu.SMEM((8, 128), jnp.int32), pltpu.SMEM((8, 128), jnp.int32),
        ] + [pltpu.VMEM(((b - a) * ENTRIES, TOK, ENC), BF16) for a, b in GROUPS] + [
            pltpu.VMEM((NX, NZ, 16, 128), BF16),
            pltpu.VMEM((TILES, ENC, 128), BF16),
            pltpu.VMEM((ENC, COLS), BF16),
            pltpu.VMEM((ENC, COLS), BF16),
            pltpu.VMEM((CHUNKS, ROWS, COLS), BF16),
            pltpu.VMEM((NX - 1, CAP * NZ, TOK, ENC), BF16),
            pltpu.VMEM((NX, CAP * NZ, TOK, ENC), BF16),
            pltpu.VMEM((NY, SLOTS, TOK, ENC), BF16),
            pltpu.VMEM((CHUNKS, SLOTS * TOK, ENC), BF16),
            pltpu.VMEM((CHUNKS, SLOTS * TOK, COLS), BF16),
            pltpu.VMEM((CHUNKS, SLOTS * TOK, COLS), BF16),
            pltpu.VMEM((SLOTS // 2, SPAN, COLS), F32),
            pltpu.VMEM((CHUNKS, ROWS, COLS), BF16),
            dma((2, NZ // 2, SUB)), dma((2, NZ // 2, SUB)),
            dma((NZ,)), dma((NZ,)),
            dma((9,)),
            dma((7,)), dma((CHUNKS,)),
            dma((NX,)), dma((NX,)),
            dma((7,)), dma((3,)), dma((NY,)),
            dma((NX, g)), dma((NX, g)),
            dma((3, p)), dma((3, p)),
            dma((NY, p)), dma((NY, p)),
            dma((CHUNKS,)), dma((CHUNKS,)),
        ],
        compiler_params=pltpu.CompilerParams(collective_id=0, has_side_effects=True),
        name="exchange_attend",
    )(cited(neighbour_ids), database_rows, tiles, queries, w_key, w_value)


def solution(mesh):
    torus = Mesh(mesh.devices.reshape(NX, NZ, NY, NC), SEQ_HEAD)
    in_specs = (
        P(SEQ_HEAD, None), P(SEQ, HEAD, None), P(SEQ, None), P(None, HEAD), P(None, HEAD), P(),
    )
    return jax.shard_map(
        per_device, mesh=torus, in_specs=in_specs, out_specs=P(SEQ_HEAD, None), check_vma=False
    )
```

```python
import jax
import jax.numpy as jnp
from jax import lax
from jax.experimental import pallas as pl
from jax.experimental.pallas import tpu as pltpu
from jax.sharding import Mesh
from jax.sharding import PartitionSpec as P

HEAD_DIM = 128
NX, NZ, NY, NC = 4, 16, 4, 2
SEQ = ("x", "z")
HEAD = ("y", "c")
SEQ_HEAD = ("x", "z", "y", "c")
MESH = pl.DeviceIdType.MESH
BF16 = jnp.bfloat16
F32 = jnp.float32

ENC = 896
ENTRIES = 8
TOK = 8
SLOTS = 22
CAP = 2
SUB = 4
WROWS = 14
COLS = 512
ROWS = 88
CHUNKS = 8
TILES = 8
LEAP = 4

GROUPS = ((0, 1),) + tuple((2 * d - 1, min(2 * d + 1, NZ)) for d in range(1, NZ // 2 + 1))

SPAN = 64
SPANS = (0, 1, 4, 5, 6, 9, 10, 2, 3, 7, 8)
PIECES = ((0, 7), (7, 11))
HALVES = ((0, 3, 4, 7), (1, 2, 5, 6))


def order_of(d, way):
    return 2 * d - 1 + way


def kernel(
    ids_hbm, db_ref, wsh_ref, q_ref, wk_ref, wv_ref, out_ref,
    few_ref, ids_ref, wsh, vtab, inv_ref, own_ref, z0, z1, z2, z3, z4, z5, z6, z7, z8, wz, wenc, wk, wv, qbuf, s_x, r_x, raw, enc, kbuf, vbuf, mixed, obuf,
    z_send, z_recv, wz_send, wz_recv, local, q_send, q_recv,
    wx_send, wx_recv, wy_send, wy_recv, wy_sib, x_send, x_recv,
    y_send, y_recv, e_send, e_recv, o_send, o_recv,
):
    x, z, y, c = (lax.axis_index(a) for a in SEQ_HEAD)
    r = 1 - 2 * c
    h = 2 * y + c
    zg = (z0, z1, z2, z3, z4, z5, z6, z7, z8)

    def wrap(v, n):
        return lax.rem(v + 2 * n, n)

    def copy(src, dst, ssem, rsem, dev):
        return pltpu.make_async_remote_copy(
            src_ref=src, dst_ref=dst, send_sem=ssem, recv_sem=rsem,
            device_id=dev, device_id_type=MESH,
        )

    sibling = (x, z, y, 1 - c)

    def at_x(dx):
        return (wrap(x + dx, NX), z, y, c)

    def at_z(dz):
        return (x, wrap(z + dz, NZ), y, c)

    def at_y(dy):
        return (x, z, wrap(y + dy, NY), c)

    others = [(0, 1)] + [(dy, e) for dy in (2, 1, 3) for e in (0, 1)]

    def at_head(dy, e):
        return (x, z, wrap(y + dy, NY), wrap(c + e, NC))

    read_ids = pltpu.make_async_copy(ids_hbm, few_ref, local.at[8])
    read_w = pltpu.make_async_copy(wsh_ref, wsh, local.at[1])
    read_w.start()
    read_ids.start()

    barrier = pltpu.get_barrier_semaphore()
    partners = [at_z(s * d) for d in range(1, LEAP + 1) for s in (1, -1)]
    partners += [at_x(n) for n in range(1, NX)] + [at_head(*o) for o in others]
    for dev in partners:
        pl.semaphore_signal(barrier, inc=1, device_id=dev, device_id_type=MESH)

    read_w.wait()
    tile = pl.multiple_of((h - lax.div(h, TILES - 1)) * 128, 128)
    wz[x, 0] = jnp.zeros((16, 128), BF16)
    wz[x, 0, :WROWS, :] = wsh[:, pl.ds(tile, 128)]
    pl.semaphore_wait(barrier, len(partners))

    sends = []

    def go(cp):
        cp.start()
        sends.append(cp)

    def w_copy(n, slot, dist):
        return copy(wz.at[x, slot], wz.at[x, slot], wz_send.at[n], wz_recv.at[slot], at_z(r * dist))

    for n, d in enumerate([s * d for d in range(1, LEAP + 1) for s in (1, -1)]):
        slot = d % NZ
        go(copy(wz.at[x, 0], wz.at[x, slot], wz_send.at[n], wz_recv.at[slot], at_z(r * d)))

    def zpiece(place, i):
        g = next(k for k, (a, b) in enumerate(GROUPS) if a <= place < b)
        n = ENTRIES // SUB
        return zg[g].at[pl.ds((place - GROUPS[g][0]) * ENTRIES + i * n, n)]

    def z_dev(way):
        return at_z(r if way == 0 else -r)

    for i in range(SUB):
        for way in range(2):
            go(copy(
                db_ref.at[pl.ds(i * (ENTRIES // SUB), ENTRIES // SUB)], zpiece(order_of(1, way), i),
                z_send.at[way, 0, i], z_recv.at[way, 0, i], z_dev(way),
            ))

    for n, (dy, e) in enumerate(others):
        dev = at_head(dy, e)
        to = 2 * dev[2] + dev[3]
        cols = pl.ds(pl.multiple_of(to * COLS, COLS), COLS)
        go(copy(q_ref.at[:, cols], qbuf.at[h], q_send.at[n], q_recv.at[h], dev))

    own_cols = pl.ds(pl.multiple_of(h * COLS, COLS), COLS)
    locals_ = [
        pltpu.make_async_copy(db_ref, z0.at[pl.ds(0, ENTRIES)], local.at[0]),
        pltpu.make_async_copy(wk_ref, wk, local.at[2]),
        pltpu.make_async_copy(wv_ref, wv, local.at[3]),
        pltpu.make_async_copy(q_ref.at[:, own_cols], qbuf.at[h], local.at[4]),
    ]
    for cp in locals_:
        cp.start()

    read_ids.wait()
    ids_ref[...] = jnp.zeros((8, 128), jnp.int32)
    ids_ref[:NX, :SLOTS] = few_ref[...]
    ids = ids_ref[...]
    lane = lax.broadcasted_iota(jnp.int32, (8, 128), 1)
    owner_of = ids >> 3
    number = jnp.zeros_like(ids)
    for k in range(1, SLOTS):
        same = (pltpu.roll(owner_of, k, 1) == owner_of) & (lane >= k)
        number = number + jnp.where(same, 1, 0)
    behind = (r * (z - (owner_of & (NZ - 1)))) & (NZ - 1)
    place_of = jnp.where(behind < NZ // 2, jnp.maximum(2 * behind - 1, 0), 2 * (NZ - behind))
    place_of = jnp.where(behind == NZ // 2, NZ - 1, place_of)
    slot_of = CAP * place_of + number
    column_of = owner_of >> 4
    key = jnp.where(column_of == x, slot_of * ENTRIES + (ids & (ENTRIES - 1)), -1)
    inverse = jnp.zeros_like(ids)
    for k in range(SLOTS):
        one = jnp.broadcast_to(key[:, k : k + 1], (8, 128))
        inverse = inverse + jnp.where((one >> 3) == lane, one & (ENTRIES - 1), 0)
    vtab[0] = inverse
    vtab[1] = slot_of * NX + column_of
    to_scalar = [
        pltpu.make_async_copy(vtab.at[0], inv_ref, local.at[6]),
        pltpu.make_async_copy(vtab.at[1], own_ref, local.at[7]),
    ]
    for cp in to_scalar:
        cp.start()

    def z_step(k):
        d = k + 1
        for i in range(SUB):
            for way in range(2):
                if d == NZ // 2 and way == 1:
                    continue
                piece = zpiece(order_of(d, way), i)
                copy(piece, piece, z_send.at[way, k, i], z_recv.at[way, k, i], z_dev(way)).wait_recv()
                if d + 1 < NZ // 2 or (d + 1 == NZ // 2 and way == 0):
                    go(copy(
                        piece, zpiece(order_of(d + 1, way), i),
                        z_send.at[way, k + 1, i], z_recv.at[way, k + 1, i], z_dev(way),
                    ))

    def w_arrived(slot):
        copy(wz.at[x, slot], wz.at[x, slot], wz_send.at[0], wz_recv.at[slot], at_z(1)).wait_recv()

    def w_leap():
        n = 2 * LEAP
        for s in (1, -1):
            held = s * LEAP % NZ
            w_arrived(held)
            for d in range(1, LEAP + 1):
                total = LEAP + d
                if total == NZ // 2 and s == -1:
                    continue
                slot = s * total % NZ
                go(copy(wz.at[x, held], wz.at[x, slot], wz_send.at[n], wz_recv.at[slot], at_z(s * r * d)))
                n += 1

    def w_columns():
        for slot in range(1, NZ):
            if slot not in (LEAP, NZ - LEAP):
                w_arrived(slot)
        for n in range(1, NX):
            go(copy(wz.at[x], wz.at[x], wx_send.at[n], wx_recv.at[x], at_x(n)))

    class Gather:
        def start(self):
            own = wenc.at[h]
            go(copy(own, own, wy_send.at[0], wy_recv.at[0], at_y(r)))
            go(copy(own, own, wy_send.at[1], wy_recv.at[1], at_y(-r)))
            go(copy(own, own, wy_send.at[2], wy_sib.at[0], sibling))

        def arrive(self, n):
            step = (-1, 1, 2)[n] * r
            piece = wenc.at[2 * wrap(y + step, NY) + c]
            copy(piece, piece, wy_send.at[0], wy_recv.at[n], at_y(r)).wait_recv()
            if n == 0:
                go(copy(piece, piece, wy_send.at[3], wy_recv.at[2], at_y(r)))
            go(copy(piece, piece, wy_send.at[4 + n], wy_sib.at[wrap(step, NY)], sibling))

        def from_sibling(self, delta):
            piece = wenc.at[2 * wrap(y + delta, NY) + 1 - c]
            copy(piece, piece, wy_send.at[0], wy_sib.at[delta], sibling).wait_recv()

    w_gather = Gather()

    def w_pack():
        for n in range(1, NX):
            src = wrap(x + n, NX)
            copy(wz.at[src], wz.at[src], wx_send.at[n], wx_recv.at[src], at_x(n)).wait_recv()
        lhs_rows, rhs_rows = ENTRIES * WROWS, NZ * 16
        row = lax.broadcasted_iota(jnp.int32, (lhs_rows, rhs_rows), 0)
        col = lax.broadcasted_iota(jnp.int32, (lhs_rows, rhs_rows), 1)
        owner = (z - r * (col >> 4)) & (NZ - 1)
        inner = col & 15
        place = owner * WROWS + inner
        for b in range(2):
            pick = jnp.where((inner < WROWS) & (place == row + b * lhs_rows), 1.0, 0.0).astype(BF16)
            for a in range(NX):
                block = wz[a].reshape(rhs_rows, 128)
                packed = jnp.dot(pick, block, preferred_element_type=F32).astype(BF16)
                wenc[h, pl.ds((2 * a + b) * lhs_rows, lhs_rows), :] = packed
        w_gather.start()

    def x_slots(g):
        return CAP * GROUPS[g][0], CAP * (GROUPS[g][1] - GROUPS[g][0])

    def x_exchange(g):
        first, count = x_slots(g)
        for n in (2, 1, 3, 0):
            dest = wrap(x + n, NX)
            for j in range(first, first + count):
                at = (j // CAP - GROUPS[g][0]) * ENTRIES + (inv_ref[dest, j] & (ENTRIES - 1))
                if n:
                    s_x[n - 1, j] = zg[g][at]
                else:
                    r_x[x, j] = zg[g][at]
            if n:
                part = pl.ds(first, count)
                go(copy(s_x.at[n - 1, part], r_x.at[x, part], x_send.at[n, g], x_recv.at[x, g], at_x(n)))

    locals_[0].wait()
    for cp in to_scalar:
        cp.wait()
    x_exchange(0)
    for k in range(NZ // 2):
        z_step(k)
        if k == 0:
            w_leap()
        x_exchange(k + 1)
        if k == 2:
            w_columns()
        if k == 4:
            w_pack()
        if k == 6:
            w_gather.arrive(0)
            w_gather.arrive(1)

    for g in range(len(GROUPS)):
        first, count = x_slots(g)
        for n in range(1, NX):
            src = wrap(x + n, NX)
            part = r_x.at[src, pl.ds(first, count)]
            copy(part, part, x_send.at[n, g], x_recv.at[src, g], at_x(n)).wait_recv()

    def slots_of(p):
        a, b = PIECES[p]
        return pl.ds(2 * a, 2 * (b - a))

    def y_part(step, p):
        return raw.at[wrap(y + step, NY), slots_of(p)]

    def y_start(p):
        own = y_part(0, p)
        go(copy(own, own, y_send.at[0, p], y_recv.at[0, p], at_y(r)))
        go(copy(own, own, y_send.at[1, p], y_recv.at[1, p], at_y(-r)))

    for p, (a, b) in enumerate(PIECES):
        for j in range(2 * a, 2 * b):
            code = own_ref[x, (j % 2) * (SLOTS // 2) + SPANS[j // 2]]
            raw[y, j] = r_x[code & (NX - 1), (code >> 2) & (CAP * NZ - 1)]
        if p == 0:
            y_start(p)

    w_gather.arrive(2)
    for n in range(NY):
        w_gather.from_sibling(n)

    def y_arrive(n, p):
        piece = y_part((-1, 1, 2)[n] * r, p)
        copy(piece, piece, y_send.at[0, p], y_recv.at[n, p], at_y(r)).wait_recv()
        if n == 0:
            go(copy(piece, piece, y_send.at[2, p], y_recv.at[2, p], at_y(r)))

    def rows_of(p):
        a, b = PIECES[p]
        return pl.ds(16 * a, 16 * (b - a)), 16 * (b - a)

    def encode(step, p):
        chip = wrap(y + step, NY)
        rows, count = rows_of(p)
        here = 2 * chip + c
        rawf = raw[chip, slots_of(p)].astype(F32).reshape(count, ENC)
        mean_square = jnp.sum(rawf * rawf, axis=-1, keepdims=True) * (1.0 / ENC)
        normed = (rawf * lax.rsqrt(mean_square + 1e-06)).astype(BF16)
        for t in range(TILES // 2):
            w2 = jnp.concatenate([wenc[2 * t], wenc[2 * t + 1]], axis=1)
            summed = jnp.dot(normed, w2, preferred_element_type=F32)
            width = min(256, ENC - 256 * t)
            summed = summed[:, :width]
            part = rawf[:, 256 * t : 256 * t + width]
            enc[here, rows, 256 * t : 256 * t + width] = (part + summed * jax.nn.sigmoid(summed)).astype(BF16)
        own = enc.at[here, rows]
        delta = wrap(step, NY)
        go(copy(own, own, e_send.at[delta, p], e_recv.at[delta, p], sibling))

    def project(step, p):
        chip = wrap(y + step, NY)
        rows, n = rows_of(p)
        theirs = enc.at[2 * chip + 1 - c, rows]
        delta = wrap(step, NY)
        copy(theirs, theirs, e_send.at[delta, p], e_recv.at[delta, p], sibling).wait_recv()
        pair = pl.ds(2 * chip, 2)
        lhs = enc[pair, rows, :].reshape(2 * n, ENC)
        for w, out in ((wk, kbuf), (wv, vbuf)):
            got = jnp.dot(lhs, w[...], preferred_element_type=F32).astype(BF16)
            out[pair, rows, :] = got.reshape(2, n, COLS)

    def attend(spans):
        heads = [slice(hd * HEAD_DIM, (hd + 1) * HEAD_DIM) for hd in range(COLS // HEAD_DIM)]
        pairs = [(span, cols) for span in spans for cols in heads]
        scores = []
        for span, cols in pairs:
            first, last = SPAN * span, SPAN * (span + 1)
            rows = []
            for chunk in range(first // ROWS, (last - 1) // ROWS + 1):
                a, b = max(first - ROWS * chunk, 0), min(last - ROWS * chunk, ROWS)
                rows.append(qbuf[chunk, :, cols].astype(F32)[a:b])
            q = jnp.concatenate(rows, axis=0).astype(BF16)
            at = 16 * SPANS.index(span)
            k = kbuf[:, at : at + 16, cols].reshape(128, HEAD_DIM)
            scores.append(lax.dot_general(q, k, (((1,), (1,)), ((), ())), preferred_element_type=F32))
        scores = jnp.concatenate(scores, axis=0) * HEAD_DIM ** (-0.5)
        weights = jnp.exp(scores - jnp.max(scores, axis=-1, keepdims=True))
        scale = 1.0 / jnp.sum(weights, axis=-1, keepdims=True)
        probs = (weights * scale).astype(BF16)
        outs = []
        for n, (span, cols) in enumerate(pairs):
            at = 16 * SPANS.index(span)
            v = vbuf[:, at : at + 16, cols].reshape(128, HEAD_DIM)
            outs.append(jnp.dot(probs[SPAN * n : SPAN * (n + 1)], v, preferred_element_type=F32))
        for out, (span, cols) in zip(outs, pairs):
            mixed[span, :, cols] = out

    def finish(chunk):
        first, last = ROWS * chunk, ROWS * (chunk + 1)
        rows = []
        for span in range(first // SPAN, (last - 1) // SPAN + 1):
            a, b = max(first - SPAN * span, 0), min(last - SPAN * span, SPAN)
            rows.append(mixed[span, a:b, :])
        obuf[chunk] = jnp.concatenate(rows, axis=0).astype(BF16)

        @pl.when(h == chunk)
        def _():
            own_out.start()

        @pl.when(h != chunk)
        def _():
            out_copy(chunk).start()

    def out_copy(chunk):
        dev = (x, z, chunk // NC, chunk % NC)
        return copy(obuf.at[chunk], out_ref.at[:, own_cols], o_send.at[chunk], o_recv.at[h], dev)

    own_out = pltpu.make_async_copy(obuf.at[h], out_ref.at[:, own_cols], local.at[5])

    encode(0, 0)
    y_arrive(0, 0)
    y_start(1)
    encode(-r, 0)
    y_arrive(1, 0)
    encode(r, 0)
    locals_[1].wait()
    locals_[2].wait()
    project(0, 0)
    encode(0, 1)
    project(r, 0)
    project(-r, 0)
    project(0, 1)
    locals_[3].wait()
    for n, (dy, e) in enumerate(others):
        src = 2 * wrap(y + dy, NY) + wrap(c + e, NC)
        copy(qbuf.at[src], qbuf.at[src], q_send.at[n], q_recv.at[src], sibling).wait_recv()
    y_arrive(2, 0)
    encode(2, 0)
    y_arrive(0, 1)
    encode(-r, 1)
    project(2, 0)
    attend((0, 1))
    finish(0)
    y_arrive(1, 1)
    encode(r, 1)
    attend((4, 5))
    finish(3)
    project(r, 1)
    attend((6,))
    finish(4)
    project(-r, 1)
    attend((9, 10))
    finish(7)
    y_arrive(2, 1)
    encode(2, 1)
    project(2, 1)
    attend((2, 3))
    finish(1)
    finish(2)
    attend((7, 8))
    finish(5)
    finish(6)

    own_out.wait()
    for dy, e in others:
        src = 2 * wrap(y + dy, NY) + wrap(c + e, NC)
        cols = pl.ds(pl.multiple_of(src * COLS, COLS), COLS)
        copy(obuf.at[h], out_ref.at[:, cols], o_send.at[src], o_recv.at[src], sibling).wait_recv()
    for cp in sends:
        cp.wait_send()
    for dy, e in others:
        copy(obuf.at[h], obuf.at[h], o_send.at[2 * wrap(y + dy, NY) + wrap(c + e, NC)], o_recv.at[h], sibling).wait_send()


def cited(neighbour_ids):
    ids = neighbour_ids.T.reshape(CAP, NX, NZ, SLOTS // 2)
    ids = lax.dynamic_index_in_dim(ids, lax.axis_index("z"), 2, keepdims=False)
    return jnp.concatenate([ids[0], ids[1]], axis=1)


def per_device(queries, database_rows, w_encoder, w_key, w_value, neighbour_ids):
    g, p = len(GROUPS), len(PIECES)
    dma = pltpu.SemaphoreType.DMA
    any_ = pl.BlockSpec(memory_space=pl.ANY)
    return pl.pallas_call(
        kernel,
        out_shape=jax.ShapeDtypeStruct(queries.shape, BF16),
        in_specs=[any_] * 6,
        out_specs=any_,
        scratch_shapes=[
            pltpu.VMEM((NX, SLOTS), jnp.int32),
            pltpu.VMEM((8, 128), jnp.int32),
            pltpu.VMEM((WROWS, ENC), BF16),
            pltpu.VMEM((2, 8, 128), jnp.int32), pltpu.SMEM((8, 128), jnp.int32), pltpu.SMEM((8, 128), jnp.int32),
        ] + [pltpu.VMEM(((b - a) * ENTRIES, TOK, ENC), BF16) for a, b in GROUPS] + [
            pltpu.VMEM((NX, NZ, 16, 128), BF16),
            pltpu.VMEM((TILES, ENC, 128), BF16),
            pltpu.VMEM((ENC, COLS), BF16),
            pltpu.VMEM((ENC, COLS), BF16),
            pltpu.VMEM((CHUNKS, ROWS, COLS), BF16),
            pltpu.VMEM((NX - 1, CAP * NZ, TOK, ENC), BF16),
            pltpu.VMEM((NX, CAP * NZ, TOK, ENC), BF16),
            pltpu.VMEM((NY, SLOTS, TOK, ENC), BF16),
            pltpu.VMEM((CHUNKS, SLOTS * TOK, ENC), BF16),
            pltpu.VMEM((CHUNKS, SLOTS * TOK, COLS), BF16),
            pltpu.VMEM((CHUNKS, SLOTS * TOK, COLS), BF16),
            pltpu.VMEM((SLOTS // 2, SPAN, COLS), F32),
            pltpu.VMEM((CHUNKS, ROWS, COLS), BF16),
            dma((2, NZ // 2, SUB)), dma((2, NZ // 2, SUB)),
            dma((NZ,)), dma((NZ,)),
            dma((9,)),
            dma((7,)), dma((CHUNKS,)),
            dma((NX,)), dma((NX,)),
            dma((7,)), dma((3,)), dma((NY,)),
            dma((NX, g)), dma((NX, g)),
            dma((3, p)), dma((3, p)),
            dma((NY, p)), dma((NY, p)),
            dma((CHUNKS,)), dma((CHUNKS,)),
        ],
        compiler_params=pltpu.CompilerParams(collective_id=0, has_side_effects=True),
        name="exchange_attend",
    )(cited(neighbour_ids), database_rows, w_encoder, queries, w_key, w_value)


def solution(mesh):
    torus = Mesh(mesh.devices.reshape(NX, NZ, NY, NC), SEQ_HEAD)
    in_specs = (
        P(SEQ_HEAD, None), P(SEQ, HEAD, None), P(SEQ, None), P(None, HEAD), P(None, HEAD), P(),
    )
    return jax.shard_map(
        per_device, mesh=torus, in_specs=in_specs, out_specs=P(SEQ_HEAD, None), check_vma=False
    )
```

```python
import jax
import jax.numpy as jnp
from jax import lax
from jax.experimental import pallas as pl
from jax.experimental.pallas import tpu as pltpu
from jax.sharding import Mesh
from jax.sharding import PartitionSpec as P

HEAD_DIM = 128
NX, NZ, NY, NC = 4, 16, 4, 2
SEQ = ("x", "z")
HEAD = ("y", "c")
SEQ_HEAD = ("x", "z", "y", "c")
MESH = pl.DeviceIdType.MESH
BF16 = jnp.bfloat16
F32 = jnp.float32

ENC = 896
ENTRIES = 8
TOK = 8
SLOTS = 22
CAP = 2
SUB = 4
WROWS = 14
COLS = 512
ROWS = 88
CHUNKS = 8
TILES = 8
LEAP = 4

GROUPS = ((0, 1),) + tuple((2 * d - 1, min(2 * d + 1, NZ)) for d in range(1, NZ // 2 + 1))

SPAN = 64
SPANS = (0, 1, 4, 5, 6, 9, 10, 2, 3, 7, 8)
PIECES = ((0, 7), (7, 11))
HALVES = ((0, 3, 4, 7), (1, 2, 5, 6))


def order_of(d, way):
    return 2 * d - 1 + way


def kernel(
    ids_hbm, db_ref, wsh_ref, q_ref, wk_ref, wv_ref, out_ref,
    few_ref, ids_ref, wsh, vtab, inv_ref, own_ref, z0, z1, z2, z3, z4, z5, z6, z7, z8, wz, wenc, wk, wv, qbuf, s_x, r_x, raw, enc, kbuf, vbuf, mixed, obuf,
    z_send, z_recv, wz_send, wz_recv, local, q_send, q_recv,
    wx_send, wx_recv, wy_send, wy_recv, wy_sib, x_send, x_recv,
    y_send, y_recv, e_send, e_recv, o_send, o_recv,
):
    x, z, y, c = (lax.axis_index(a) for a in SEQ_HEAD)
    r = 1 - 2 * c
    h = 2 * y + c
    zg = (z0, z1, z2, z3, z4, z5, z6, z7, z8)

    def wrap(v, n):
        return lax.rem(v + 2 * n, n)

    def copy(src, dst, ssem, rsem, dev):
        return pltpu.make_async_remote_copy(
            src_ref=src, dst_ref=dst, send_sem=ssem, recv_sem=rsem,
            device_id=dev, device_id_type=MESH,
        )

    sibling = (x, z, y, 1 - c)

    def at_x(dx):
        return (wrap(x + dx, NX), z, y, c)

    def at_z(dz):
        return (x, wrap(z + dz, NZ), y, c)

    def at_y(dy):
        return (x, z, wrap(y + dy, NY), c)

    others = [(0, 1)] + [(dy, e) for dy in (2, 1, 3) for e in (0, 1)]

    def at_head(dy, e):
        return (x, z, wrap(y + dy, NY), wrap(c + e, NC))

    read_ids = pltpu.make_async_copy(ids_hbm, few_ref, local.at[8])
    read_w = pltpu.make_async_copy(wsh_ref, wsh, local.at[1])
    read_w.start()
    read_ids.start()

    barrier = pltpu.get_barrier_semaphore()
    partners = [at_z(s * d) for d in range(1, LEAP + 1) for s in (1, -1)]
    partners += [at_x(n) for n in range(1, NX)] + [at_head(*o) for o in others]
    for dev in partners:
        pl.semaphore_signal(barrier, inc=1, device_id=dev, device_id_type=MESH)

    read_w.wait()
    tile = pl.multiple_of((h - lax.div(h, TILES - 1)) * 128, 128)
    wz[x, 0] = jnp.zeros((16, 128), BF16)
    wz[x, 0, :WROWS, :] = wsh[:, pl.ds(tile, 128)]
    pl.semaphore_wait(barrier, len(partners))

    def sent(ref, sem):
        copy(ref, ref, sem, q_recv.at[0], sibling).wait_send()

    def arrived(ref, sem):
        copy(ref, ref, q_send.at[0], sem, sibling).wait_recv()

    def lane_of(slot):
        return {LEAP: 0, NZ - LEAP: 1}.get(slot, 2)

    for d in [s * d for d in range(1, LEAP + 1) for s in (1, -1)]:
        slot = d % NZ
        copy(wz.at[x, 0], wz.at[x, slot], wz_send.at[0], wz_recv.at[lane_of(slot)], at_z(r * d)).start()

    def zpiece(place, i):
        g = next(k for k, (a, b) in enumerate(GROUPS) if a <= place < b)
        n = ENTRIES // SUB
        return zg[g].at[pl.ds((place - GROUPS[g][0]) * ENTRIES + i * n, n)]

    def z_dev(way):
        return at_z(r if way == 0 else -r)

    for i in range(SUB):
        for way in range(2):
            copy(
                db_ref.at[pl.ds(i * (ENTRIES // SUB), ENTRIES // SUB)], zpiece(order_of(1, way), i),
                z_send.at[way], z_recv.at[way, 0, i], z_dev(way),
            ).start()

    for dy, e in others:
        dev = at_head(dy, e)
        to = 2 * dev[2] + dev[3]
        cols = pl.ds(pl.multiple_of(to * COLS, COLS), COLS)
        copy(q_ref.at[:, cols], qbuf.at[h], q_send.at[0], q_recv.at[0], dev).start()

    own_cols = pl.ds(pl.multiple_of(h * COLS, COLS), COLS)
    locals_ = [
        pltpu.make_async_copy(db_ref, z0.at[pl.ds(0, ENTRIES)], local.at[0]),
        pltpu.make_async_copy(wk_ref, wk, local.at[2]),
        pltpu.make_async_copy(wv_ref, wv, local.at[3]),
        pltpu.make_async_copy(q_ref.at[:, own_cols], qbuf.at[h], local.at[4]),
    ]
    for cp in locals_:
        cp.start()

    read_ids.wait()
    ids_ref[...] = jnp.zeros((8, 128), jnp.int32)
    ids_ref[:NX, :SLOTS] = few_ref[...]
    ids = ids_ref[...]
    lane = lax.broadcasted_iota(jnp.int32, (8, 128), 1)
    owner_of = ids >> 3
    number = jnp.zeros_like(ids)
    for k in range(1, SLOTS):
        same = (pltpu.roll(owner_of, k, 1) == owner_of) & (lane >= k)
        number = number + jnp.where(same, 1, 0)
    behind = (r * (z - (owner_of & (NZ - 1)))) & (NZ - 1)
    place_of = jnp.where(behind < NZ // 2, jnp.maximum(2 * behind - 1, 0), 2 * (NZ - behind))
    place_of = jnp.where(behind == NZ // 2, NZ - 1, place_of)
    slot_of = CAP * place_of + number
    column_of = owner_of >> 4
    key = jnp.where(column_of == x, slot_of * ENTRIES + (ids & (ENTRIES - 1)), -1)
    inverse = jnp.zeros_like(ids)
    for k in range(SLOTS):
        one = jnp.broadcast_to(key[:, k : k + 1], (8, 128))
        inverse = inverse + jnp.where((one >> 3) == lane, one & (ENTRIES - 1), 0)
    vtab[0] = inverse
    vtab[1] = slot_of * NX + column_of
    to_scalar = [
        pltpu.make_async_copy(vtab.at[0], inv_ref, local.at[6]),
        pltpu.make_async_copy(vtab.at[1], own_ref, local.at[7]),
    ]
    for cp in to_scalar:
        cp.start()

    def z_step(k):
        d = k + 1
        for i in range(SUB):
            for way in range(2):
                if d == NZ // 2 and way == 1:
                    continue
                piece = zpiece(order_of(d, way), i)
                copy(piece, piece, z_send.at[way], z_recv.at[way, k, i], z_dev(way)).wait_recv()
                if d + 1 < NZ // 2 or (d + 1 == NZ // 2 and way == 0):
                    copy(
                        piece, zpiece(order_of(d + 1, way), i),
                        z_send.at[way], z_recv.at[way, k + 1, i], z_dev(way),
                    ).start()

    def w_leap():
        for s in (1, -1):
            held = s * LEAP % NZ
            arrived(wz.at[x, held], wz_recv.at[lane_of(held)])
            for d in range(1, LEAP + 1):
                total = LEAP + d
                if total == NZ // 2 and s == -1:
                    continue
                slot = s * total % NZ
                copy(wz.at[x, held], wz.at[x, slot], wz_send.at[0], wz_recv.at[lane_of(slot)], at_z(s * r * d)).start()

    def w_columns():
        arrived(wz.at[x, pl.ds(0, NZ - 3)], wz_recv.at[2])
        for n in range(1, NX):
            copy(wz.at[x], wz.at[x], wx_send.at[0], wx_recv.at[0], at_x(n)).start()

    class Gather:
        def start(self):
            own = wenc.at[h]
            copy(own, own, wy_send.at[0], wy_recv.at[0], at_y(r)).start()
            copy(own, own, wy_send.at[0], wy_recv.at[1], at_y(-r)).start()
            copy(own, own, wy_send.at[0], wy_sib.at[0], sibling).start()

        def arrive(self, n):
            step = (-1, 1, 2)[n] * r
            piece = wenc.at[2 * wrap(y + step, NY) + c]
            copy(piece, piece, wy_send.at[0], wy_recv.at[n], at_y(r)).wait_recv()
            if n == 0:
                copy(piece, piece, wy_send.at[0], wy_recv.at[2], at_y(r)).start()
            copy(piece, piece, wy_send.at[0], wy_sib.at[0], sibling).start()

    w_gather = Gather()

    def w_pack():
        arrived(wz.at[pl.ds(0, NX - 1)], wx_recv.at[0])
        lhs_rows, rhs_rows = ENTRIES * WROWS, NZ * 16
        row = lax.broadcasted_iota(jnp.int32, (lhs_rows, rhs_rows), 0)
        col = lax.broadcasted_iota(jnp.int32, (lhs_rows, rhs_rows), 1)
        owner = (z - r * (col >> 4)) & (NZ - 1)
        inner = col & 15
        place = owner * WROWS + inner
        for b in range(2):
            pick = jnp.where((inner < WROWS) & (place == row + b * lhs_rows), 1.0, 0.0).astype(BF16)
            for a in range(NX):
                block = wz[a].reshape(rhs_rows, 128)
                packed = jnp.dot(pick, block, preferred_element_type=F32).astype(BF16)
                wenc[h, pl.ds((2 * a + b) * lhs_rows, lhs_rows), :] = packed
        w_gather.start()

    def x_slots(g):
        return CAP * GROUPS[g][0], CAP * (GROUPS[g][1] - GROUPS[g][0])

    def x_exchange(g):
        first, count = x_slots(g)
        for n in (2, 1, 3, 0):
            dest = wrap(x + n, NX)
            for j in range(first, first + count):
                at = (j // CAP - GROUPS[g][0]) * ENTRIES + (inv_ref[dest, j] & (ENTRIES - 1))
                if n:
                    s_x[n - 1, j] = zg[g][at]
                else:
                    r_x[x, j] = zg[g][at]
            if n:
                part = pl.ds(first, count)
                copy(s_x.at[n - 1, part], r_x.at[x, part], x_send.at[0], x_recv.at[0], at_x(n)).start()

    locals_[0].wait()
    for cp in to_scalar:
        cp.wait()
    x_exchange(0)
    for k in range(NZ // 2):
        z_step(k)
        if k == 0:
            w_leap()
        x_exchange(k + 1)
        if k == 2:
            w_columns()
        if k == 4:
            w_pack()
        if k == 6:
            w_gather.arrive(0)
            w_gather.arrive(1)

    arrived(s_x, x_recv.at[0])

    def slots_of(p):
        a, b = PIECES[p]
        return pl.ds(2 * a, 2 * (b - a))

    def y_part(step, p):
        return raw.at[wrap(y + step, NY), slots_of(p)]

    def y_start(p):
        own = y_part(0, p)
        copy(own, own, y_send.at[0], y_recv.at[0, p], at_y(r)).start()
        copy(own, own, y_send.at[0], y_recv.at[1, p], at_y(-r)).start()

    for p, (a, b) in enumerate(PIECES):
        for j in range(2 * a, 2 * b):
            code = own_ref[x, (j % 2) * (SLOTS // 2) + SPANS[j // 2]]
            raw[y, j] = r_x[code & (NX - 1), (code >> 2) & (CAP * NZ - 1)]
        if p == 0:
            y_start(p)

    w_gather.arrive(2)
    arrived(wenc.at[pl.ds(0, NY)], wy_sib.at[0])

    def y_arrive(n, p):
        piece = y_part((-1, 1, 2)[n] * r, p)
        copy(piece, piece, y_send.at[0], y_recv.at[n, p], at_y(r)).wait_recv()
        if n == 0:
            copy(piece, piece, y_send.at[0], y_recv.at[2, p], at_y(r)).start()

    def rows_of(p):
        a, b = PIECES[p]
        return pl.ds(16 * a, 16 * (b - a)), 16 * (b - a)

    def encode(step, p):
        chip = wrap(y + step, NY)
        rows, count = rows_of(p)
        here = 2 * chip + c
        rawf = raw[chip, slots_of(p)].astype(F32).reshape(count, ENC)
        mean_square = jnp.sum(rawf * rawf, axis=-1, keepdims=True) * (1.0 / ENC)
        normed = (rawf * lax.rsqrt(mean_square + 1e-06)).astype(BF16)
        for t in range(TILES // 2):
            w2 = jnp.concatenate([wenc[2 * t], wenc[2 * t + 1]], axis=1)
            summed = jnp.dot(normed, w2, preferred_element_type=F32)
            width = min(256, ENC - 256 * t)
            summed = summed[:, :width]
            part = rawf[:, 256 * t : 256 * t + width]
            enc[here, rows, 256 * t : 256 * t + width] = (part + summed * jax.nn.sigmoid(summed)).astype(BF16)
        own = enc.at[here, rows]
        delta = wrap(step, NY)
        copy(own, own, e_send.at[0], e_recv.at[delta, p], sibling).start()

    def project(step, p):
        chip = wrap(y + step, NY)
        rows, n = rows_of(p)
        theirs = enc.at[2 * chip + 1 - c, rows]
        delta = wrap(step, NY)
        copy(theirs, theirs, e_send.at[0], e_recv.at[delta, p], sibling).wait_recv()
        pair = pl.ds(2 * chip, 2)
        lhs = enc[pair, rows, :].reshape(2 * n, ENC)
        for w, out in ((wk, kbuf), (wv, vbuf)):
            got = jnp.dot(lhs, w[...], preferred_element_type=F32).astype(BF16)
            out[pair, rows, :] = got.reshape(2, n, COLS)

    def attend(spans):
        heads = [slice(hd * HEAD_DIM, (hd + 1) * HEAD_DIM) for hd in range(COLS // HEAD_DIM)]
        pairs = [(span, cols) for span in spans for cols in heads]
        scores = []
        for span, cols in pairs:
            first, last = SPAN * span, SPAN * (span + 1)
            rows = []
            for chunk in range(first // ROWS, (last - 1) // ROWS + 1):
                a, b = max(first - ROWS * chunk, 0), min(last - ROWS * chunk, ROWS)
                rows.append(qbuf[chunk, :, cols].astype(F32)[a:b])
            q = jnp.concatenate(rows, axis=0).astype(BF16)
            at = 16 * SPANS.index(span)
            k = kbuf[:, at : at + 16, cols].reshape(128, HEAD_DIM)
            scores.append(lax.dot_general(q, k, (((1,), (1,)), ((), ())), preferred_element_type=F32))
        scores = jnp.concatenate(scores, axis=0) * HEAD_DIM ** (-0.5)
        weights = jnp.exp(scores - jnp.max(scores, axis=-1, keepdims=True))
        scale = 1.0 / jnp.sum(weights, axis=-1, keepdims=True)
        probs = (weights * scale).astype(BF16)
        outs = []
        for n, (span, cols) in enumerate(pairs):
            at = 16 * SPANS.index(span)
            v = vbuf[:, at : at + 16, cols].reshape(128, HEAD_DIM)
            outs.append(jnp.dot(probs[SPAN * n : SPAN * (n + 1)], v, preferred_element_type=F32))
        for out, (span, cols) in zip(outs, pairs):
            mixed[span, :, cols] = out

    def finish(chunk):
        first, last = ROWS * chunk, ROWS * (chunk + 1)
        rows = []
        for span in range(first // SPAN, (last - 1) // SPAN + 1):
            a, b = max(first - SPAN * span, 0), min(last - SPAN * span, SPAN)
            rows.append(mixed[span, a:b, :])
        obuf[chunk] = jnp.concatenate(rows, axis=0).astype(BF16)

        @pl.when(h == chunk)
        def _():
            own_out.start()

        @pl.when(h != chunk)
        def _():
            out_copy(chunk).start()

    def out_copy(chunk):
        dev = (x, z, chunk // NC, chunk % NC)
        return copy(obuf.at[chunk], out_ref.at[:, own_cols], o_send.at[0], o_recv.at[0], dev)

    own_out = pltpu.make_async_copy(obuf.at[h], out_ref.at[:, own_cols], local.at[5])

    encode(0, 0)
    y_arrive(0, 0)
    y_start(1)
    encode(-r, 0)
    y_arrive(1, 0)
    encode(r, 0)
    locals_[1].wait()
    locals_[2].wait()
    project(0, 0)
    encode(0, 1)
    project(r, 0)
    project(-r, 0)
    project(0, 1)
    locals_[3].wait()
    arrived(qbuf.at[pl.ds(0, CHUNKS - 1)], q_recv.at[0])
    y_arrive(2, 0)
    encode(2, 0)
    y_arrive(0, 1)
    encode(-r, 1)
    project(2, 0)
    attend((0, 1))
    finish(0)
    y_arrive(1, 1)
    encode(r, 1)
    attend((4, 5))
    finish(3)
    project(r, 1)
    attend((6,))
    finish(4)
    project(-r, 1)
    attend((9, 10))
    finish(7)
    y_arrive(2, 1)
    encode(2, 1)
    project(2, 1)
    attend((2, 3))
    finish(1)
    finish(2)
    attend((7, 8))
    finish(5)
    finish(6)

    own_out.wait()
    some = pl.ds(0, CHUNKS - 1)
    arrived(obuf.at[some], o_recv.at[0])
    sent(obuf.at[some], o_send.at[0])
    sent(qbuf.at[some], q_send.at[0])
    sent(r_x.at[pl.ds(0, 2)], z_send.at[0])
    sent(r_x.at[:, pl.ds(0, 14)], z_send.at[1])
    sent(wz.at[0, pl.ds(0, NZ - 1)], wz_send.at[0])
    sent(wz.at[pl.ds(0, NX - 1)], wx_send.at[0])
    sent(wenc.at[pl.ds(0, TILES - 1)], wy_send.at[0])
    sent(s_x, x_send.at[0])
    sent(raw.at[pl.ds(0, NY - 1)], y_send.at[0])
    sent(enc.at[pl.ds(0, NY)], e_send.at[0])


def cited(neighbour_ids):
    ids = neighbour_ids.T.reshape(CAP, NX, NZ, SLOTS // 2)
    ids = lax.dynamic_index_in_dim(ids, lax.axis_index("z"), 2, keepdims=False)
    return jnp.concatenate([ids[0], ids[1]], axis=1)


def per_device(queries, database_rows, w_encoder, w_key, w_value, neighbour_ids):
    p = len(PIECES)
    dma = pltpu.SemaphoreType.DMA
    any_ = pl.BlockSpec(memory_space=pl.ANY)
    return pl.pallas_call(
        kernel,
        out_shape=jax.ShapeDtypeStruct(queries.shape, BF16),
        in_specs=[any_] * 6,
        out_specs=any_,
        scratch_shapes=[
            pltpu.VMEM((NX, SLOTS), jnp.int32),
            pltpu.VMEM((8, 128), jnp.int32),
            pltpu.VMEM((WROWS, ENC), BF16),
            pltpu.VMEM((2, 8, 128), jnp.int32), pltpu.SMEM((8, 128), jnp.int32), pltpu.SMEM((8, 128), jnp.int32),
        ] + [pltpu.VMEM(((b - a) * ENTRIES, TOK, ENC), BF16) for a, b in GROUPS] + [
            pltpu.VMEM((NX, NZ, 16, 128), BF16),
            pltpu.VMEM((TILES, ENC, 128), BF16),
            pltpu.VMEM((ENC, COLS), BF16),
            pltpu.VMEM((ENC, COLS), BF16),
            pltpu.VMEM((CHUNKS, ROWS, COLS), BF16),
            pltpu.VMEM((NX - 1, CAP * NZ, TOK, ENC), BF16),
            pltpu.VMEM((NX, CAP * NZ, TOK, ENC), BF16),
            pltpu.VMEM((NY, SLOTS, TOK, ENC), BF16),
            pltpu.VMEM((CHUNKS, SLOTS * TOK, ENC), BF16),
            pltpu.VMEM((CHUNKS, SLOTS * TOK, COLS), BF16),
            pltpu.VMEM((CHUNKS, SLOTS * TOK, COLS), BF16),
            pltpu.VMEM((SLOTS // 2, SPAN, COLS), F32),
            pltpu.VMEM((CHUNKS, ROWS, COLS), BF16),
            dma((2,)), dma((2, NZ // 2, SUB)),
            dma((1,)), dma((3,)),
            dma((9,)),
            dma((1,)), dma((1,)),
            dma((1,)), dma((1,)),
            dma((1,)), dma((3,)), dma((1,)),
            dma((1,)), dma((1,)),
            dma((1,)), dma((3, p)),
            dma((1,)), dma((NY, p)),
            dma((1,)), dma((1,)),
        ],
        compiler_params=pltpu.CompilerParams(collective_id=0, has_side_effects=True),
        name="exchange_attend",
    )(cited(neighbour_ids), database_rows, w_encoder, queries, w_key, w_value)


def solution(mesh):
    torus = Mesh(mesh.devices.reshape(NX, NZ, NY, NC), SEQ_HEAD)
    in_specs = (
        P(SEQ_HEAD, None), P(SEQ, HEAD, None), P(SEQ, None), P(None, HEAD), P(None, HEAD), P(),
    )
    return jax.shard_map(
        per_device, mesh=torus, in_specs=in_specs, out_specs=P(SEQ_HEAD, None), check_vma=False
    )
```

```python
import jax
import jax.numpy as jnp
from jax import lax
from jax.experimental import pallas as pl
from jax.experimental.pallas import tpu as pltpu
from jax.sharding import Mesh
from jax.sharding import PartitionSpec as P

HEAD_DIM = 128
NX, NZ, NY, NC = 4, 16, 4, 2
SEQ = ("x", "z")
HEAD = ("y", "c")
SEQ_HEAD = ("x", "z", "y", "c")
MESH = pl.DeviceIdType.MESH
BF16 = jnp.bfloat16
F32 = jnp.float32

ENC = 896
ENTRIES = 8
TOK = 8
SLOTS = 22
CAP = 2
SUB = 4
WROWS = 14
COLS = 512
ROWS = 88
CHUNKS = 8
TILES = 8
LEAP = 2
LEAPS = (NZ // 2 - 1) // LEAP

GROUPS = ((0, 1),) + tuple((2 * d - 1, min(2 * d + 1, NZ)) for d in range(1, NZ // 2 + 1))

SPAN = 64
SPANS = (0, 1, 4, 5, 6, 9, 10, 2, 3, 7, 8)
PIECES = ((0, 7), (7, 11))
HALVES = ((0, 3, 4, 7), (1, 2, 5, 6))


def order_of(d, way):
    return 2 * d - 1 + way


def kernel(
    ids_hbm, db_ref, wsh_ref, q_ref, wk_ref, wv_ref, out_ref,
    few_ref, ids_ref, wsh, vtab, inv_ref, own_ref, z0, z1, z2, z3, z4, z5, z6, z7, z8, wz, wenc, wk, wv, qbuf, s_x, r_x, raw, enc, kbuf, vbuf, mixed, obuf,
    z_send, z_recv, wz_send, wz_recv, local, q_send, q_recv,
    wx_send, wx_recv, wy_send, wy_recv, wy_sib, x_send, x_recv,
    y_send, y_recv, e_send, e_recv, o_send, o_recv,
):
    x, z, y, c = (lax.axis_index(a) for a in SEQ_HEAD)
    r = 1 - 2 * c
    h = 2 * y + c
    zg = (z0, z1, z2, z3, z4, z5, z6, z7, z8)

    def wrap(v, n):
        return lax.rem(v + 2 * n, n)

    def copy(src, dst, ssem, rsem, dev):
        return pltpu.make_async_remote_copy(
            src_ref=src, dst_ref=dst, send_sem=ssem, recv_sem=rsem,
            device_id=dev, device_id_type=MESH,
        )

    sibling = (x, z, y, 1 - c)

    def at_x(dx):
        return (wrap(x + dx, NX), z, y, c)

    def at_z(dz):
        return (x, wrap(z + dz, NZ), y, c)

    def at_y(dy):
        return (x, z, wrap(y + dy, NY), c)

    others = [(0, 1)] + [(dy, e) for dy in (2, 1, 3) for e in (0, 1)]

    def at_head(dy, e):
        return (x, z, wrap(y + dy, NY), wrap(c + e, NC))

    read_ids = pltpu.make_async_copy(ids_hbm, few_ref, local.at[8])
    read_w = pltpu.make_async_copy(wsh_ref, wsh, local.at[1])
    read_w.start()
    read_ids.start()

    barrier = pltpu.get_barrier_semaphore()
    partners = [at_z(s * d) for d in range(1, LEAP + 1) for s in (1, -1)]
    partners += [at_x(n) for n in range(1, NX)] + [at_head(*o) for o in others]
    for dev in partners:
        pl.semaphore_signal(barrier, inc=1, device_id=dev, device_id_type=MESH)

    read_w.wait()
    tile = pl.multiple_of((h - lax.div(h, TILES - 1)) * 128, 128)
    wz[x, 0] = jnp.zeros((16, 128), BF16)
    wz[x, 0, :WROWS, :] = wsh[:, pl.ds(tile, 128)]
    pl.semaphore_wait(barrier, len(partners))

    def sent(ref, sem):
        copy(ref, ref, sem, q_recv.at[0], sibling).wait_send()

    def arrived(ref, sem):
        copy(ref, ref, q_send.at[0], sem, sibling).wait_recv()

    def lane_of(slot):
        for n in range(LEAPS):
            if slot in (LEAP * (n + 1), NZ - LEAP * (n + 1)):
                return 2 * n + (slot > NZ // 2)
        return 2 * LEAPS

    for d in [s * d for d in range(1, LEAP + 1) for s in (1, -1)]:
        slot = d % NZ
        copy(wz.at[x, 0], wz.at[x, slot], wz_send.at[0], wz_recv.at[lane_of(slot)], at_z(r * d)).start()

    def zpiece(place, i):
        g = next(k for k, (a, b) in enumerate(GROUPS) if a <= place < b)
        n = ENTRIES // SUB
        return zg[g].at[pl.ds((place - GROUPS[g][0]) * ENTRIES + i * n, n)]

    def z_dev(way):
        return at_z(r if way == 0 else -r)

    for i in range(SUB):
        for way in range(2):
            copy(
                db_ref.at[pl.ds(i * (ENTRIES // SUB), ENTRIES // SUB)], zpiece(order_of(1, way), i),
                z_send.at[way], z_recv.at[way, 0, i], z_dev(way),
            ).start()

    for dy, e in others:
        dev = at_head(dy, e)
        to = 2 * dev[2] + dev[3]
        cols = pl.ds(pl.multiple_of(to * COLS, COLS), COLS)
        copy(q_ref.at[:, cols], qbuf.at[h], q_send.at[0], q_recv.at[0], dev).start()

    own_cols = pl.ds(pl.multiple_of(h * COLS, COLS), COLS)
    locals_ = [
        pltpu.make_async_copy(db_ref, z0.at[pl.ds(0, ENTRIES)], local.at[0]),
        pltpu.make_async_copy(wk_ref, wk, local.at[2]),
        pltpu.make_async_copy(wv_ref, wv, local.at[3]),
        pltpu.make_async_copy(q_ref.at[:, own_cols], qbuf.at[h], local.at[4]),
    ]
    for cp in locals_:
        cp.start()

    read_ids.wait()
    ids_ref[...] = jnp.zeros((8, 128), jnp.int32)
    ids_ref[:NX, :SLOTS] = few_ref[...]
    ids = ids_ref[...]
    lane = lax.broadcasted_iota(jnp.int32, (8, 128), 1)
    owner_of = ids >> 3
    number = jnp.zeros_like(ids)
    for k in range(1, SLOTS):
        same = (pltpu.roll(owner_of, k, 1) == owner_of) & (lane >= k)
        number = number + jnp.where(same, 1, 0)
    behind = (r * (z - (owner_of & (NZ - 1)))) & (NZ - 1)
    place_of = jnp.where(behind < NZ // 2, jnp.maximum(2 * behind - 1, 0), 2 * (NZ - behind))
    place_of = jnp.where(behind == NZ // 2, NZ - 1, place_of)
    slot_of = CAP * place_of + number
    column_of = owner_of >> 4
    key = jnp.where(column_of == x, slot_of * ENTRIES + (ids & (ENTRIES - 1)), -1)
    inverse = jnp.zeros_like(ids)
    for k in range(SLOTS):
        one = jnp.broadcast_to(key[:, k : k + 1], (8, 128))
        inverse = inverse + jnp.where((one >> 3) == lane, one & (ENTRIES - 1), 0)
    vtab[0] = inverse
    vtab[1] = slot_of * NX + column_of
    to_scalar = [
        pltpu.make_async_copy(vtab.at[0], inv_ref, local.at[6]),
        pltpu.make_async_copy(vtab.at[1], own_ref, local.at[7]),
    ]
    for cp in to_scalar:
        cp.start()

    def z_step(k):
        d = k + 1
        for i in range(SUB):
            for way in range(2):
                if d == NZ // 2 and way == 1:
                    continue
                piece = zpiece(order_of(d, way), i)
                copy(piece, piece, z_send.at[way], z_recv.at[way, k, i], z_dev(way)).wait_recv()
                if d + 1 < NZ // 2 or (d + 1 == NZ // 2 and way == 0):
                    copy(
                        piece, zpiece(order_of(d + 1, way), i),
                        z_send.at[way], z_recv.at[way, k + 1, i], z_dev(way),
                    ).start()

    def w_leap(number):
        for s in (1, -1):
            held = s * LEAP * number % NZ
            arrived(wz.at[x, held], wz_recv.at[lane_of(held)])
            for d in range(1, LEAP + 1):
                total = LEAP * number + d
                if total > NZ // 2 or (total == NZ // 2 and s == -1):
                    continue
                slot = s * total % NZ
                copy(wz.at[x, held], wz.at[x, slot], wz_send.at[0], wz_recv.at[lane_of(slot)], at_z(s * r * d)).start()

    def w_columns():
        arrived(wz.at[x, pl.ds(0, NZ - 1 - 2 * LEAPS)], wz_recv.at[2 * LEAPS])
        for n in range(1, NX):
            copy(wz.at[x], wz.at[x], wx_send.at[0], wx_recv.at[0], at_x(n)).start()

    class Gather:
        def start(self):
            own = wenc.at[h]
            copy(own, own, wy_send.at[0], wy_recv.at[0], at_y(r)).start()
            copy(own, own, wy_send.at[0], wy_recv.at[1], at_y(-r)).start()
            copy(own, own, wy_send.at[0], wy_sib.at[0], sibling).start()

        def arrive(self, n):
            step = (-1, 1, 2)[n] * r
            piece = wenc.at[2 * wrap(y + step, NY) + c]
            copy(piece, piece, wy_send.at[0], wy_recv.at[n], at_y(r)).wait_recv()
            if n == 0:
                copy(piece, piece, wy_send.at[0], wy_recv.at[2], at_y(r)).start()
            copy(piece, piece, wy_send.at[0], wy_sib.at[0], sibling).start()

    w_gather = Gather()

    def w_pack():
        arrived(wz.at[pl.ds(0, NX - 1)], wx_recv.at[0])
        lhs_rows, rhs_rows = ENTRIES * WROWS, NZ * 16
        row = lax.broadcasted_iota(jnp.int32, (lhs_rows, rhs_rows), 0)
        col = lax.broadcasted_iota(jnp.int32, (lhs_rows, rhs_rows), 1)
        owner = (z - r * (col >> 4)) & (NZ - 1)
        inner = col & 15
        place = owner * WROWS + inner
        for b in range(2):
            pick = jnp.where((inner < WROWS) & (place == row + b * lhs_rows), 1.0, 0.0).astype(BF16)
            for a in range(NX):
                block = wz[a].reshape(rhs_rows, 128)
                packed = jnp.dot(pick, block, preferred_element_type=F32).astype(BF16)
                wenc[h, pl.ds((2 * a + b) * lhs_rows, lhs_rows), :] = packed
        w_gather.start()

    def x_slots(g):
        return CAP * GROUPS[g][0], CAP * (GROUPS[g][1] - GROUPS[g][0])

    def x_exchange(g):
        first, count = x_slots(g)
        for n in (2, 1, 3, 0):
            dest = wrap(x + n, NX)
            for j in range(first, first + count):
                at = (j // CAP - GROUPS[g][0]) * ENTRIES + (inv_ref[dest, j] & (ENTRIES - 1))
                if n:
                    s_x[n - 1, j] = zg[g][at]
                else:
                    r_x[x, j] = zg[g][at]
            if n:
                part = pl.ds(first, count)
                copy(s_x.at[n - 1, part], r_x.at[x, part], x_send.at[0], x_recv.at[0], at_x(n)).start()

    locals_[0].wait()
    for cp in to_scalar:
        cp.wait()
    x_exchange(0)
    for k in range(NZ // 2):
        z_step(k)
        if k < LEAPS:
            w_leap(k + 1)
        x_exchange(k + 1)
        if k == 3:
            w_columns()
        if k == 5:
            w_pack()
        if k == 7:
            w_gather.arrive(0)
            w_gather.arrive(1)

    arrived(s_x, x_recv.at[0])

    def slots_of(p):
        a, b = PIECES[p]
        return pl.ds(2 * a, 2 * (b - a))

    def y_part(step, p):
        return raw.at[wrap(y + step, NY), slots_of(p)]

    def y_start(p):
        own = y_part(0, p)
        copy(own, own, y_send.at[0], y_recv.at[0, p], at_y(r)).start()
        copy(own, own, y_send.at[0], y_recv.at[1, p], at_y(-r)).start()

    for p, (a, b) in enumerate(PIECES):
        for j in range(2 * a, 2 * b):
            code = own_ref[x, (j % 2) * (SLOTS // 2) + SPANS[j // 2]]
            raw[y, j] = r_x[code & (NX - 1), (code >> 2) & (CAP * NZ - 1)]
        if p == 0:
            y_start(p)

    w_gather.arrive(2)
    arrived(wenc.at[pl.ds(0, NY)], wy_sib.at[0])

    def y_arrive(n, p):
        piece = y_part((-1, 1, 2)[n] * r, p)
        copy(piece, piece, y_send.at[0], y_recv.at[n, p], at_y(r)).wait_recv()
        if n == 0:
            copy(piece, piece, y_send.at[0], y_recv.at[2, p], at_y(r)).start()

    def rows_of(p):
        a, b = PIECES[p]
        return pl.ds(16 * a, 16 * (b - a)), 16 * (b - a)

    def encode(steps, p):
        rows, count = rows_of(p)
        chips = [wrap(y + step, NY) for step in steps]
        rawf = jnp.concatenate(
            [raw[chip, slots_of(p)].astype(F32).reshape(count, ENC) for chip in chips], axis=0
        )
        mean_square = jnp.sum(rawf * rawf, axis=-1, keepdims=True) * (1.0 / ENC)
        normed = (rawf * lax.rsqrt(mean_square + 1e-06)).astype(BF16)
        for t in range(TILES // 2):
            w2 = jnp.concatenate([wenc[2 * t], wenc[2 * t + 1]], axis=1)
            summed = jnp.dot(normed, w2, preferred_element_type=F32)
            width = min(256, ENC - 256 * t)
            summed = summed[:, :width]
            part = rawf[:, 256 * t : 256 * t + width]
            coded = (part + summed * jax.nn.sigmoid(summed)).astype(BF16)
            for n, chip in enumerate(chips):
                enc[2 * chip + c, rows, 256 * t : 256 * t + width] = coded[n * count : (n + 1) * count]
        for step, chip in zip(steps, chips):
            own = enc.at[2 * chip + c, rows]
            copy(own, own, e_send.at[0], e_recv.at[wrap(step, NY), p], sibling).start()

    def project(steps, p):
        rows, n = rows_of(p)
        pairs = []
        for step in steps:
            chip = wrap(y + step, NY)
            theirs = enc.at[2 * chip + 1 - c, rows]
            copy(theirs, theirs, e_send.at[0], e_recv.at[wrap(step, NY), p], sibling).wait_recv()
            pairs.append(pl.ds(2 * chip, 2))
        lhs = jnp.concatenate([enc[pair, rows, :].reshape(2 * n, ENC) for pair in pairs], axis=0)
        for w, out in ((wk, kbuf), (wv, vbuf)):
            got = jnp.dot(lhs, w[...], preferred_element_type=F32).astype(BF16)
            for m, pair in enumerate(pairs):
                out[pair, rows, :] = got[2 * n * m : 2 * n * (m + 1)].reshape(2, n, COLS)

    def attend(spans):
        heads = [slice(hd * HEAD_DIM, (hd + 1) * HEAD_DIM) for hd in range(COLS // HEAD_DIM)]
        pairs = [(span, cols) for span in spans for cols in heads]
        scores = []
        for span, cols in pairs:
            first, last = SPAN * span, SPAN * (span + 1)
            rows = []
            for chunk in range(first // ROWS, (last - 1) // ROWS + 1):
                a, b = max(first - ROWS * chunk, 0), min(last - ROWS * chunk, ROWS)
                rows.append(qbuf[chunk, :, cols].astype(F32)[a:b])
            q = jnp.concatenate(rows, axis=0).astype(BF16)
            at = 16 * SPANS.index(span)
            k = kbuf[:, at : at + 16, cols].reshape(128, HEAD_DIM)
            scores.append(lax.dot_general(q, k, (((1,), (1,)), ((), ())), preferred_element_type=F32))
        scores = jnp.concatenate(scores, axis=0) * HEAD_DIM ** (-0.5)
        weights = jnp.exp(scores - jnp.max(scores, axis=-1, keepdims=True))
        scale = 1.0 / jnp.sum(weights, axis=-1, keepdims=True)
        probs = (weights * scale).astype(BF16)
        outs = []
        for n, (span, cols) in enumerate(pairs):
            at = 16 * SPANS.index(span)
            v = vbuf[:, at : at + 16, cols].reshape(128, HEAD_DIM)
            outs.append(jnp.dot(probs[SPAN * n : SPAN * (n + 1)], v, preferred_element_type=F32))
        for out, (span, cols) in zip(outs, pairs):
            mixed[span, :, cols] = out

    def finish(chunk):
        first, last = ROWS * chunk, ROWS * (chunk + 1)
        rows = []
        for span in range(first // SPAN, (last - 1) // SPAN + 1):
            a, b = max(first - SPAN * span, 0), min(last - SPAN * span, SPAN)
            rows.append(mixed[span, a:b, :])
        obuf[chunk] = jnp.concatenate(rows, axis=0).astype(BF16)

        @pl.when(h == chunk)
        def _():
            own_out.start()

        @pl.when(h != chunk)
        def _():
            out_copy(chunk).start()

    def out_copy(chunk):
        dev = (x, z, chunk // NC, chunk % NC)
        return copy(obuf.at[chunk], out_ref.at[:, own_cols], o_send.at[0], o_recv.at[0], dev)

    own_out = pltpu.make_async_copy(obuf.at[h], out_ref.at[:, own_cols], local.at[5])

    encode((0,), 0)
    encode((0,), 1)
    locals_[1].wait()
    locals_[2].wait()
    y_arrive(0, 0)
    y_start(1)
    y_arrive(1, 0)
    encode((-r, r), 0)
    project((0,), 0)
    project((0,), 1)
    project((-r, r), 0)
    locals_[3].wait()
    arrived(qbuf.at[pl.ds(0, CHUNKS - 1)], q_recv.at[0])
    y_arrive(2, 0)
    encode((2,), 0)
    y_arrive(0, 1)
    y_arrive(1, 1)
    encode((-r, r), 1)
    project((2,), 0)
    attend((0, 1))
    finish(0)
    attend((4, 5))
    finish(3)
    project((-r, r), 1)
    attend((6,))
    finish(4)
    y_arrive(2, 1)
    encode((2,), 1)
    attend((9, 10))
    finish(7)
    project((2,), 1)
    attend((2, 3))
    finish(1)
    finish(2)
    attend((7, 8))
    finish(5)
    finish(6)

    own_out.wait()
    some = pl.ds(0, CHUNKS - 1)
    arrived(obuf.at[some], o_recv.at[0])
    sent(obuf.at[some], o_send.at[0])
    sent(qbuf.at[some], q_send.at[0])
    sent(r_x.at[pl.ds(0, 2)], z_send.at[0])
    sent(r_x.at[:, pl.ds(0, 14)], z_send.at[1])
    sent(wz.at[0, pl.ds(0, NZ - 1)], wz_send.at[0])
    sent(wz.at[pl.ds(0, NX - 1)], wx_send.at[0])
    sent(wenc.at[pl.ds(0, TILES - 1)], wy_send.at[0])
    sent(s_x, x_send.at[0])
    sent(raw.at[pl.ds(0, NY - 1)], y_send.at[0])
    sent(enc.at[pl.ds(0, NY)], e_send.at[0])


def cited(neighbour_ids):
    ids = neighbour_ids.T.reshape(CAP, NX, NZ, SLOTS // 2)
    ids = lax.dynamic_index_in_dim(ids, lax.axis_index("z"), 2, keepdims=False)
    return jnp.concatenate([ids[0], ids[1]], axis=1)


def per_device(queries, database_rows, w_encoder, w_key, w_value, neighbour_ids):
    p = len(PIECES)
    dma = pltpu.SemaphoreType.DMA
    any_ = pl.BlockSpec(memory_space=pl.ANY)
    return pl.pallas_call(
        kernel,
        out_shape=jax.ShapeDtypeStruct(queries.shape, BF16),
        in_specs=[any_] * 6,
        out_specs=any_,
        scratch_shapes=[
            pltpu.VMEM((NX, SLOTS), jnp.int32),
            pltpu.VMEM((8, 128), jnp.int32),
            pltpu.VMEM((WROWS, ENC), BF16),
            pltpu.VMEM((2, 8, 128), jnp.int32), pltpu.SMEM((8, 128), jnp.int32), pltpu.SMEM((8, 128), jnp.int32),
        ] + [pltpu.VMEM(((b - a) * ENTRIES, TOK, ENC), BF16) for a, b in GROUPS] + [
            pltpu.VMEM((NX, NZ, 16, 128), BF16),
            pltpu.VMEM((TILES, ENC, 128), BF16),
            pltpu.VMEM((ENC, COLS), BF16),
            pltpu.VMEM((ENC, COLS), BF16),
            pltpu.VMEM((CHUNKS, ROWS, COLS), BF16),
            pltpu.VMEM((NX - 1, CAP * NZ, TOK, ENC), BF16),
            pltpu.VMEM((NX, CAP * NZ, TOK, ENC), BF16),
            pltpu.VMEM((NY, SLOTS, TOK, ENC), BF16),
            pltpu.VMEM((CHUNKS, SLOTS * TOK, ENC), BF16),
            pltpu.VMEM((CHUNKS, SLOTS * TOK, COLS), BF16),
            pltpu.VMEM((CHUNKS, SLOTS * TOK, COLS), BF16),
            pltpu.VMEM((SLOTS // 2, SPAN, COLS), F32),
            pltpu.VMEM((CHUNKS, ROWS, COLS), BF16),
            dma((2,)), dma((2, NZ // 2, SUB)),
            dma((1,)), dma((2 * LEAPS + 1,)),
            dma((9,)),
            dma((1,)), dma((1,)),
            dma((1,)), dma((1,)),
            dma((1,)), dma((3,)), dma((1,)),
            dma((1,)), dma((1,)),
            dma((1,)), dma((3, p)),
            dma((1,)), dma((NY, p)),
            dma((1,)), dma((1,)),
        ],
        compiler_params=pltpu.CompilerParams(collective_id=0, has_side_effects=True),
        name="exchange_attend",
    )(cited(neighbour_ids), database_rows, w_encoder, queries, w_key, w_value)


def solution(mesh):
    torus = Mesh(mesh.devices.reshape(NX, NZ, NY, NC), SEQ_HEAD)
    in_specs = (
        P(SEQ_HEAD, None), P(SEQ, HEAD, None), P(SEQ, None), P(None, HEAD), P(None, HEAD), P(),
    )
    return jax.shard_map(
        per_device, mesh=torus, in_specs=in_specs, out_specs=P(SEQ_HEAD, None), check_vma=False
    )
```
